256 devices in a mesh: req: 32 (over x, y, core), exp: 8 (over z).
Axes of the slice: x: 4, y: 4, z: 8, core: 2. Of those that a mesh axis runs over, the one named last changes fastest.
Arguments:
- residual: bfloat16 [4096, 2048], P(('req', 'exp')), may hold values from -12 to 12
- queries: bfloat16 [4096, 2, 2048], P('req', None, 'exp'), may hold values from -9 to 9
- kv_cache: bfloat16 [608, 2, 128, 2048], P('req', None, None, 'exp'), may hold values from -4 to 4
- page_table: int32 [288, 11], P('req'), may hold values from 0 to 18, as said below
- seq_lengths: int32 [288], P('req'), may hold values from 8 to 1408, as said below
- head_route: int32 [4096, 2], P('req'), may hold values from 0 to 7, all different within a row
- head_gate: float32 [4096, 2], P('req'), may hold values from 0.2 to 1
- out_weight: bfloat16 [8, 2048, 2048], P(None, 'exp'), may hold values from -0.5 to 0.5
- norm_gain: float32 [2048], replicated, may hold values from 0.25 to 1.75
- expert_route: int32 [4096, 2], P(('req', 'exp')), may hold values from 0 to 7, all different within a row; in each aligned block of 16 rows (0 to 15, 16 to 31, ...) at most 8 rows name the same one
- expert_gate: float32 [4096, 2], P(('req', 'exp')), may hold values from 0.2 to 1
- gate_up: bfloat16 [8, 2, 2048, 5632], P('exp', None, None, 'req'), may hold values from -0.125 to 0.125
- down_weight: bfloat16 [8, 5632, 2048], P('exp', 'req'), may hold values from -0.078125 to 0.078125
Outputs:
- attended: bfloat16 [4096, 2048], P(('req', 'exp'))
- expert_mix: bfloat16 [4096, 2048], P(('req', 'exp'))
The draws below stay inside these ranges and needn't reach their ends.
Inputs may be any that keep to these rules, and one draw needn't show every extreme that they name: `page_table`: pages are numbered within the slot's group. A group's slot 0 lists 11 different pages; each other slot repeats one page along its row; no two slots of a group share a page. `seq_lengths`: slot 0 of every group is a prefill request of length at least 120; the other slots are decode requests of length at most 128. `head_route`: each row names 2 different attention experts. `expert_route`: each row names 2 different experts; within the rows of one device no expert is named by more than 8 rows.
All inputs are finite; a program needn't handle non-finite values.
Results may differ from the reference program's by a relative error of at most 0.023.
Values may be sent and summed in bfloat16 or wider, within the bound.
A program may use at most 128 MiB of HBM per device.

```python
import math
import jax
import jax.numpy as jnp
import numpy as np
from jax import lax

D = 2048
H = 16
HD = 128
AEXP = 8
FF = 5632
TOPA = 2
PAGE = 128
MAXP = 11
NDEC = 8
SPAN = 120
FEXP = 8
TOK_GRP = 128
ROWS_DEV = 16
CAP = 8
TOKENS = 4096
SLOTS = 9
POOL = 19
POOL_ALL = 608
N_REQ = 32
N_EXP = 8


def draw_queries(key, part):
    shape = (TOKENS, TOPA, H * HD)
    own_key = jax.random.fold_in(key, 11)
    base = jnp.clip(jax.random.normal(own_key, shape, jnp.float32), -4.0, 4.0)
    return base.astype(jnp.bfloat16)


def draw_kv_cache(key, part):
    shape = (POOL_ALL, 2, PAGE, H * HD)
    own_key = jax.random.fold_in(key, 13)
    base = jnp.clip(jax.random.normal(own_key, shape, jnp.float32), -4.0, 4.0)
    return base.astype(jnp.bfloat16)


def draw_residual(key, part):
    shape = (TOKENS, D)
    scales = jnp.exp(jax.random.uniform(jax.random.fold_in(key, 17), (TOKENS, 1), jnp.float32, math.log(0.3), math.log(3.0)))
    own_key = jax.random.fold_in(key, 19)
    base = jnp.clip(jax.random.normal(own_key, shape, jnp.float32), -4.0, 4.0)
    return (base * scales).astype(jnp.bfloat16)


def permute_pool(pool_key):
    return jax.random.permutation(pool_key, POOL)


def page_layout(key):
    base_key = jax.random.fold_in(key, 23)
    pool_keys = jax.random.split(jax.random.fold_in(base_key, 1), N_REQ)
    orders = jax.vmap(permute_pool)(pool_keys).astype(jnp.int32)
    prefill_len = jax.random.randint(jax.random.fold_in(base_key, 2), (N_REQ,), SPAN, MAXP * PAGE + 1, dtype=jnp.int32)
    longest = jax.random.randint(jax.random.fold_in(base_key, 3), (), 0, N_REQ, dtype=jnp.int32)
    prefill_len = prefill_len.at[longest].set(MAXP * PAGE)
    decode_len = jax.random.randint(jax.random.fold_in(base_key, 4), (N_REQ, NDEC), 8, PAGE + 1, dtype=jnp.int32)
    fullest = jax.random.randint(jax.random.fold_in(base_key, 5), (), 0, N_REQ, dtype=jnp.int32)
    decode_len = decode_len.at[fullest, 0].set(PAGE)
    shortest = jax.random.randint(jax.random.fold_in(base_key, 6), (), 0, N_REQ, dtype=jnp.int32)
    decode_len = decode_len.at[shortest, NDEC - 1].set(8)
    lengths = jnp.concatenate([prefill_len[:, None], decode_len], axis=1).reshape(-1)
    prefill_rows = orders[:, :MAXP]
    decode_rows = jnp.broadcast_to(orders[:, MAXP:, None], (N_REQ, NDEC, MAXP))
    table = jnp.concatenate([prefill_rows[:, None, :], decode_rows], axis=1).reshape(N_REQ * SLOTS, MAXP)
    return (table, lengths)


def draw_page_table(key, part):
    return page_layout(key)[0]


def draw_seq_lengths(key, part):
    return page_layout(key)[1]


def shard_levels(rng, shape, shards, low, top_value):
    loudness = 1.0
    for dim, shards_of in shards:
        steps = jax.random.uniform(jax.random.fold_in(jax.random.fold_in(rng, 6), dim), (shards_of,), jnp.float32, low / len(shards), top_value / len(shards))
        loudness = loudness * jnp.repeat(jnp.exp(steps), shape[dim] // shards_of).reshape((-1,) + (1,) * (len(shape) - 1 - dim))
    return loudness


def choose_distinct(stream_key, rows, count, top, lift):
    order = jax.random.permutation(jax.random.fold_in(stream_key, 1), count)
    boost = order
    for power in range(3):
        boost = boost * boost // count
    boost = boost * lift // count
    tickets = jax.random.randint(jax.random.fold_in(stream_key, 2), (rows, count), 0, 4096) + boost
    holders = jax.random.permutation(jax.random.fold_in(stream_key, 3), rows)[jnp.arange(count) % rows]
    tickets = jnp.where(jnp.arange(rows)[:, None] == holders[None, :], 1 << 14, tickets)
    score = tickets * count + jnp.arange(count)
    return lax.top_k(score.astype(jnp.int32), top)[1].astype(jnp.int32)


def shared_out(rng, own, number, rows, count, top, limit, lean):
    ranking = jax.random.permutation(rng, count)
    crowded, usual = shares(count, rows * top, limit, lean, True), shares(count, rows * top, limit, lean, False)
    places = jnp.arange(count)

    def named(tallies, rotation):
        used = int((tallies > 0).sum())
        fixed = max(1, used // 4)
        passed = fixed + (places - fixed + rotation * (used - fixed)) % max(1, count - fixed)
        return jnp.zeros((count,), jnp.int32).at[ranking[jnp.where(places < fixed, places, passed)]].set(jnp.asarray(tallies, jnp.int32))

    tallies = jnp.where(number % 4 == 0, named(crowded, number // 4), named(usual, number - number // 4 - 1))
    mixed = jax.random.permutation(jax.random.fold_in(own, 3), count)
    source_of, taker = mixed[0:count // 2 * 2:2], mixed[1:count // 2 * 2:2]
    margin = jnp.minimum(tallies[source_of] - 1, limit - tallies[taker]) // 2
    margin = jnp.where((source_of == ranking[0]) | (taker == ranking[0]) | (tallies[taker] == 0), 0, jnp.maximum(margin, 0))
    passed = jax.random.randint(jax.random.fold_in(own, 4), (count // 2,), 0, 1 << 20) % (margin + 1)
    tallies = tallies.at[source_of].add(-passed).at[taker].add(passed)
    members = jnp.searchsorted(jnp.cumsum(tallies), jnp.arange(rows * top), side="right").astype(jnp.int32)
    table = members.reshape(top, rows).T
    table = table[jax.random.permutation(jax.random.fold_in(own, 1), rows)]
    rotation = jax.random.randint(jax.random.fold_in(own, 2), (rows, 1), 0, top)
    return jnp.take_along_axis(table, (jnp.arange(top)[None, :] + rotation) % top, axis=1)


def shares(count, total, bound, lean, full):
    weights = [(1 << 20) // math.isqrt(grade ** lean) + 1 for grade in range(1, count + 1)]
    largest = bound if full else min(bound, max(-(-total // count), total * weights[0] // sum(weights)))
    least = 1 if total - largest >= count - 1 else 0
    given, spare = [largest] + [least] * (count - 1), total - largest - least * (count - 1)
    while spare > 0:
        candidates = [i for i in range(1, count) if given[i] < largest] or [i for i in range(1, count) if given[i] < bound]
        whole, left = sum([weights[i] for i in candidates]), spare
        for i in candidates:
            extra = min(bound - given[i], max(1, left * weights[i] // whole), spare)
            given[i] = given[i] + extra
            spare = spare - extra
    return np.array(given)


def scatter_about(stream_key, extent, spread, bound, cuts=(), held_as=jnp.bfloat16):
    loudness = shard_levels(stream_key, extent, cuts, -0.22, 0.18) if cuts else 1.0
    result = jax.random.normal(stream_key, extent, jnp.float32) * spread * loudness
    return jnp.minimum(jnp.maximum(result, -bound), bound).astype(held_as)


def setup_inputs(seed: int = 0) -> dict:
    arg_keys = jax.random.split(jax.random.key(seed), 14)
    residual = draw_residual(jax.random.fold_in(arg_keys[13], 71), 0)
    queries = draw_queries(jax.random.fold_in(arg_keys[13], 71), 0)
    kv_cache = draw_kv_cache(jax.random.fold_in(arg_keys[13], 71), 0)
    page_table = draw_page_table(jax.random.fold_in(arg_keys[13], 71), 0)
    seq_lengths = draw_seq_lengths(jax.random.fold_in(arg_keys[13], 71), 0)
    head_route = choose_distinct(arg_keys[5], TOKENS, AEXP, TOPA, 2048)
    head_gate = jnp.clip(0.2 + 0.8 * jax.random.uniform(arg_keys[6], (TOKENS, TOPA), jnp.float32) ** shard_levels(arg_keys[6], (TOKENS, TOPA), ((0, 32),), -0.2, 0.2), 0.2, 1.0)
    out_weight = scatter_about(arg_keys[7], (AEXP, H * HD, D), HD ** -0.5, 0.5, ((1, 8),))
    norm_gain = jnp.clip(1.0 + 0.15 * jax.random.normal(arg_keys[8], (D,), jnp.float32), 0.25, 1.75)
    expert_route_keys = jax.random.split(jax.random.fold_in(arg_keys[9], 1), TOKENS // ROWS_DEV)
    expert_route_turns = jax.random.permutation(jax.random.fold_in(arg_keys[9], 3), TOKENS // ROWS_DEV)
    expert_route = jax.vmap(lambda own, number: shared_out(jax.random.fold_in(arg_keys[9], 2), own, number, ROWS_DEV, FEXP, TOPA, CAP, 2))(expert_route_keys, expert_route_turns).reshape((TOKENS, TOPA))
    expert_gate = jnp.clip(0.2 + 0.8 * jax.random.uniform(arg_keys[10], (TOKENS, TOPA), jnp.float32) ** shard_levels(arg_keys[10], (TOKENS, TOPA), ((0, 256),), -0.2, 0.2), 0.2, 1.0)
    gate_up = scatter_about(arg_keys[11], (FEXP, 2, D, FF), D ** -0.5, 0.125, ((0, 8), (3, 32)))
    down_weight = scatter_about(arg_keys[12], (FEXP, FF, D), FF ** -0.5, 0.078125, ((0, 8), (1, 32)))
    return {"residual": residual, "queries": queries, "kv_cache": kv_cache, "page_table": page_table, "seq_lengths": seq_lengths, "head_route": head_route, "head_gate": head_gate, "out_weight": out_weight, "norm_gain": norm_gain, "expert_route": expert_route, "expert_gate": expert_gate, "gate_up": gate_up, "down_weight": down_weight}


def attend(queries_one, key_rows, value_rows, positions):
    amount = queries_one.shape[0]
    heads_q = queries_one.reshape(amount * TOPA, H, HD).astype(jnp.float32)
    heads_k = key_rows.reshape(-1, H, HD).astype(jnp.float32)
    heads_v = value_rows.reshape(-1, H, HD).astype(jnp.float32)
    scores = jnp.einsum('qhd,khd->hqk', heads_q, heads_k) * HD ** (-0.5)
    key_pos = jnp.arange(heads_k.shape[0], dtype=jnp.int32)
    row_pos = jnp.repeat(positions, TOPA)
    allowed = key_pos[None, :] <= row_pos[:, None]
    scores = jnp.where(allowed[None], scores, -1e+30)
    row_max = lax.optimization_barrier(jnp.max(scores, axis=2, keepdims=True))
    raised = jnp.exp(scores - row_max)
    attention_weights = (raised / lax.optimization_barrier(jnp.sum(raised, axis=2, keepdims=True))).astype(jnp.bfloat16)
    mixture = jnp.einsum('hqk,khd->qhd', attention_weights.astype(jnp.float32), heads_v)
    return mixture.astype(jnp.bfloat16).reshape(amount, TOPA, H * HD)

def attend_group(packed):
    queries_grp, cache_grp, table_grp, lengths_grp = packed
    page_rows = cache_grp[table_grp[0]]
    key_rows = page_rows[:, 0].reshape(MAXP * PAGE, H * HD)
    value_rows = page_rows[:, 1].reshape(MAXP * PAGE, H * HD)
    first_pos = lengths_grp[0] - SPAN
    prefill_pos = first_pos + jnp.arange(SPAN, dtype=jnp.int32)
    prefill_out = attend(queries_grp[:SPAN], key_rows, value_rows, prefill_pos)
    decode_pages = cache_grp[table_grp[1:, 0]]

    def decode_one(query_row, page_block, length):
        return attend(query_row[None], page_block[0], page_block[1], (length - 1)[None])[0]
    decode_out = jax.vmap(decode_one)(queries_grp[SPAN:], decode_pages, lengths_grp[1:])
    return jnp.concatenate([prefill_out, decode_out], axis=0)

def reference(residual, queries, kv_cache, page_table, seq_lengths, head_route, head_gate, out_weight, norm_gain, expert_route, expert_gate, gate_up, down_weight):
    packed = (queries.reshape(N_REQ, TOK_GRP, TOPA, H * HD), kv_cache.reshape(N_REQ, POOL, 2, PAGE, H * HD), page_table.reshape(N_REQ, SLOTS, MAXP), seq_lengths.reshape(N_REQ, SLOTS))
    mixture = lax.map(attend_group, packed).reshape(TOKENS, TOPA, H * HD)
    heads_out = jnp.zeros((TOKENS, D), jnp.float32)
    for expert_index in range(AEXP):
        picked = head_route == expert_index
        chosen = lax.optimization_barrier(jnp.sum(jnp.where(picked[:, :, None], mixture, jnp.zeros_like(mixture)), axis=1))
        weight = lax.optimization_barrier(jnp.sum(jnp.where(picked, head_gate, jnp.zeros_like(head_gate)), axis=1))
        heads_out = heads_out + weight[:, None] * jnp.dot(chosen, out_weight[expert_index], preferred_element_type=jnp.float32)
    attended = (residual.astype(jnp.float32) + heads_out).astype(jnp.bfloat16)
    values_f = attended.astype(jnp.float32)
    normed = (values_f * lax.rsqrt(lax.optimization_barrier(jnp.mean(values_f * values_f, axis=1, keepdims=True)) + 1e-06) * norm_gain).astype(jnp.bfloat16)
    row_bound = N_REQ * N_EXP * CAP
    flat_route = expert_route.reshape(-1)
    padded = jnp.concatenate([normed, jnp.zeros((1, D), normed.dtype)], axis=0)
    gate_pad = jnp.concatenate([expert_gate.reshape(-1), jnp.zeros((1,), expert_gate.dtype)])
    mix_rows = jnp.zeros((TOKENS + 1, D), jnp.float32)
    for expert_index in range(FEXP):
        pair_index = jnp.nonzero(flat_route == expert_index, size=row_bound, fill_value=TOKENS * TOPA)[0].astype(jnp.int32)
        owners = pair_index // TOPA
        gathered = padded[owners]
        gate_part = jnp.dot(gathered, gate_up[expert_index, 0], preferred_element_type=jnp.float32)
        up_part = jnp.dot(gathered, gate_up[expert_index, 1], preferred_element_type=jnp.float32)
        active = (jax.nn.silu(gate_part) * up_part).astype(jnp.bfloat16)
        summed = jnp.dot(active, down_weight[expert_index], preferred_element_type=jnp.float32)
        expert_out = lax.optimization_barrier(summed.astype(jnp.bfloat16)).astype(jnp.float32)
        mix_rows = mix_rows.at[owners].add(gate_pad[pair_index][:, None] * expert_out)
    expert_mix = mix_rows[:TOKENS].astype(jnp.bfloat16)
    return (attended, expert_mix)
```

```python
import jax
import jax.numpy as jnp
from jax import lax
from jax.experimental import pallas as pl
from jax.experimental.pallas import tpu as pltpu
from jax.sharding import PartitionSpec as P

HD = 128
TOPA = 2
SPAN = 120
F32 = jnp.float32
BF16 = jnp.bfloat16
MESH = pl.DeviceIdType.MESH
VMEM_LIMIT = 60 * 1024 * 1024


def attention_kernel(
    table, lengths, q_ref, route_ref, gate_ref, kv_hbm, w_hbm, out_ref,
    kv, w, mix, x_rows, kv_sem, w_sem,
):
    pages = table.shape[1]
    decodes = table.shape[0] - 1
    page = kv.shape[2]
    experts = w.shape[0]
    width = q_ref.shape[2]
    tokens = q_ref.shape[1]
    head_count = width // HD
    copies = []
    for p in range(pages):
        copies.append(pltpu.make_async_copy(kv_hbm.at[table[0, p]], kv.at[p], kv_sem.at[p]))
    for s in range(decodes):
        copies.append(
            pltpu.make_async_copy(
                kv_hbm.at[table[s + 1, 0]], kv.at[pages + s], kv_sem.at[pages + s]
            )
        )
    for copy in copies:
        copy.start()
    w_copies = [pltpu.make_async_copy(w_hbm.at[e], w.at[e], w_sem.at[e]) for e in range(experts)]
    for copy in w_copies:
        copy.start()
    for copy in copies:
        copy.wait()

    def attend(q, k, v, allowed):
        scores = lax.dot_general(
            q, k, (((1,), (1,)), ((), ())), preferred_element_type=F32
        ) * HD ** (-0.5)
        scores = jnp.where(allowed, scores, -1e30)
        raised = jnp.exp(scores - jnp.max(scores, axis=1, keepdims=True))
        total = jnp.sum(raised, axis=1, keepdims=True)
        return jnp.dot(raised.astype(BF16), v, preferred_element_type=F32) / total

    keys = pages * page
    row_pos = lengths[0] - SPAN + lax.broadcasted_iota(jnp.int32, (tokens, keys), 0)
    causal = lax.broadcasted_iota(jnp.int32, (tokens, keys), 1) <= row_pos
    tail = 2 * decodes
    d_keys = decodes * page
    d_row = lax.broadcasted_iota(jnp.int32, (TOPA * tail, d_keys), 0) % tail - decodes
    d_col = lax.broadcasted_iota(jnp.int32, (TOPA * tail, d_keys), 1)
    d_slot = d_col // page
    length_of = jnp.zeros((TOPA * tail, d_keys), jnp.int32)
    for s in range(decodes):
        length_of = jnp.where(d_slot == s, lengths[s + 1], length_of)
    d_allowed = (d_slot == d_row) & (d_col % page < length_of)
    for h in range(head_count):
        cols = slice(h * HD, (h + 1) * HD)
        k_pre = kv[0:pages, 0, :, cols].reshape(keys, HD)
        v_pre = kv[0:pages, 1, :, cols].reshape(keys, HD)
        for t in range(TOPA):
            mix[t, :, cols] = attend(q_ref[t, :, cols], k_pre, v_pre, causal)
        k_dec = kv[pages : pages + decodes, 0, :, cols].reshape(d_keys, HD)
        v_dec = kv[pages : pages + decodes, 1, :, cols].reshape(d_keys, HD)
        q_dec = jnp.concatenate(
            [q_ref[t, tokens - tail : tokens, cols] for t in range(TOPA)], axis=0
        )
        o_dec = attend(q_dec, k_dec, v_dec, d_allowed)
        for t in range(TOPA):
            mix[t, SPAN:tokens, cols] = o_dec[t * tail + decodes : (t + 1) * tail]
    mixes = [mix[t].astype(BF16).astype(F32) for t in range(TOPA)]
    routes = [route_ref[:, t : t + 1] for t in range(TOPA)]
    gates = [gate_ref[:, t : t + 1] for t in range(TOPA)]
    for e in range(experts):
        gated = jnp.zeros((tokens, width), F32)
        for t in range(TOPA):
            gated = gated + jnp.where(routes[t] == e, gates[t], 0.0) * mixes[t]
        x_rows[:, e * width : (e + 1) * width] = gated.astype(BF16)
    for copy in w_copies:
        copy.wait()
    outs = w.shape[2]
    step = 512
    for n in range(0, outs, step):
        out_ref[:, n : n + step] = jnp.dot(
            x_rows[...],
            w[:, :, n : n + step].reshape(experts * width, step),
            preferred_element_type=F32,
        ).astype(BF16)


def attention(table, lengths, q, route, gate, kv_cache, out_weight):
    pool, _, page, width = kv_cache.shape
    experts, _, outs = out_weight.shape
    tokens = q.shape[1]
    vmem = pl.BlockSpec(memory_space=pltpu.VMEM)
    smem = pl.BlockSpec(memory_space=pltpu.SMEM)
    hbm = pl.BlockSpec(memory_space=pl.ANY)
    slots = table.shape[1] + table.shape[0] - 1
    return pl.pallas_call(
        attention_kernel,
        out_shape=jax.ShapeDtypeStruct((tokens, outs), BF16),
        in_specs=[smem, smem, vmem, vmem, vmem, hbm, hbm],
        out_specs=vmem,
        scratch_shapes=[
            pltpu.VMEM((slots, 2, page, width), BF16),
            pltpu.VMEM((experts, width, outs), BF16),
            pltpu.VMEM((TOPA, tokens, width), F32),
            pltpu.VMEM((tokens, experts * width), BF16),
            pltpu.SemaphoreType.DMA((slots,)),
            pltpu.SemaphoreType.DMA((experts,)),
        ],
        compiler_params=pltpu.CompilerParams(vmem_limit_bytes=VMEM_LIMIT),
        name="attention",
    )(table, lengths, q, route, gate, kv_cache, out_weight)


def layer_kernel(
    partial, residual, gain, route, egate, g_hbm, u_hbm, d_hbm, attended_ref, mix_ref,
    rs_buf, out_buf, in_buf, ra, rb, wg, wu, wd, act, pa, pb,
    ta1, ta2, sa, ta3, tb1, tb2, tb3, ret_out, ret_in,
    z_send, z_recv, ag_send, ag_recv, rs_send, rs_recv, w_send, w_recv, l_sem,
):
    nz = partial.shape[0]
    rows = residual.shape[0]
    cap = out_buf.shape[1]
    block = nz * cap
    half_cols = ra.shape[3]
    hidden = g_hbm.shape[0]
    me = lax.axis_index("req")
    z = lax.axis_index("exp")
    c = lax.rem(me, 2)
    y = lax.rem(lax.div(me, 2), 4)
    x = lax.div(me, 8)
    xp, xm, x2 = lax.rem(x + 1, 4), lax.rem(x + 3, 4), lax.rem(x + 2, 4)
    yw = y + 1 - 2 * lax.rem(y, 2)
    turned = lax.rem(y + 3, 4)
    ys = lax.rem(turned, 2)
    yo = 1 - ys
    yr = lax.rem(turned + 1 - 2 * ys + 1, 4)

    def dev(x_, y_, c_):
        return ((x_ * 4 + y_) * 2 + c_, z)

    right, left = dev(xp, y, c), dev(xm, y, c)
    pair = dev(x, yr, c)
    w_pair = dev(x, yw, c)
    core = dev(x, y, 1 - c)

    def ahead(d):
        return (me, lax.rem(z + d, nz))

    def behind(d):
        return (me, lax.rem(z + nz - d, nz))

    barrier = pltpu.get_barrier_semaphore()
    others = [ahead(d) for d in range(1, nz)] + [right, left, pair, w_pair, core]
    for other in others:
        pl.semaphore_signal(barrier, inc=1, device_id=other, device_id_type=MESH)
    pl.semaphore_wait(barrier, len(others))

    started = []

    def send(src, dst, sems, i, device):
        copy = pltpu.make_async_remote_copy(
            src_ref=src, dst_ref=dst, send_sem=sems[0].at[i], recv_sem=sems[1].at[i],
            device_id=device, device_id_type=MESH,
        )
        copy.start()
        started.append(copy)
        return copy

    zs, ags, rss, ws = (z_send, z_recv), (ag_send, ag_recv), (rs_send, rs_recv), (w_send, w_recv)

    scatter = [
        send(partial.at[lax.rem(z + d, nz)], rs_buf.at[d - 1], zs, d - 1, ahead(d))
        for d in (4, 3, 5, 2, 6, 1, 7)
    ]
    sources, stores = (g_hbm, u_hbm, d_hbm), (wg, wu, wd)

    def part(store, b):
        return store.at[pl.ds(b * hidden, hidden)]

    w_y = [send(sources[i], part(stores[i], 1), ws, i, w_pair) for i in range(3)]
    w_c = [send(sources[i], part(stores[i], 2), ws, 3 + i, core) for i in range(3)]
    w_l = [
        pltpu.make_async_copy(sources[i], part(stores[i], 0), l_sem.at[i]) for i in range(3)
    ]
    for copy in w_l:
        copy.start()

    def routed(t):
        rel = route[:, t : t + 1] - z
        rel = jnp.where(rel < 0, rel + nz, rel)
        return rel == lax.broadcasted_iota(jnp.int32, (rows, block), 1) // cap

    named = [routed(t) for t in range(TOPA)]
    member = jnp.where(named[0] | named[1], 1.0, 0.0).astype(F32)
    lower = jnp.where(
        lax.broadcasted_iota(jnp.int32, (rows, rows), 1)
        < lax.broadcasted_iota(jnp.int32, (rows, rows), 0),
        1.0, 0.0,
    ).astype(BF16)
    rank = jnp.dot(lower, member.astype(BF16), preferred_element_type=F32)
    place = (lax.broadcasted_iota(jnp.int32, (rows, block), 1) % cap).astype(F32)
    placing = jnp.where(rank == place, member, 0.0)

    for copy in scatter:
        copy.wait_recv()
    summed = residual[...].astype(F32) + partial[z].astype(F32)
    for d in range(nz - 1):
        summed = summed + rs_buf[d].astype(F32)
    attended = summed.astype(BF16)
    attended_ref[...] = attended
    values = attended.astype(F32)
    normed = (
        values
        * lax.rsqrt(jnp.mean(values * values, axis=1, keepdims=True) + 1e-06)
        * gain[...]
    ).astype(BF16)
    outgoing = lax.dot_general(
        placing.astype(BF16), normed, (((0,), (0,)), ((), ())), preferred_element_type=F32
    )
    for d in range(nz):
        out_buf[d] = outgoing[d * cap : (d + 1) * cap].astype(BF16)
    dispatch = [
        send(out_buf.at[d], in_buf.at[d - 1], zs, 6 + d, ahead(d)) for d in (4, 3, 5, 2, 6, 1, 7)
    ]
    for copy in dispatch:
        copy.wait_recv()
    arrived = jnp.concatenate(
        [out_buf[0].astype(F32)] + [in_buf[d].astype(F32) for d in range(nz - 1)], axis=0
    ).astype(BF16)

    ra[ys, x] = arrived[:, :half_cols]
    rb[ys, x] = arrived[:, half_cols:]
    mid = block // 2
    a_y = send(ra.at[ys, x], ra.at[ys, x], ags, 0, pair)
    b_r = send(rb.at[ys, x], rb.at[ys, x], ags, 1, right)
    b_l = send(rb.at[ys, x], rb.at[ys, x], ags, 2, left)
    a_y.wait_recv()
    a_r = send(ra.at[:, x], ra.at[:, x], ags, 3, right)
    a_l = send(ra.at[:, x], ra.at[:, x], ags, 4, left)
    b_r.wait_recv()
    b_r2 = send(rb.at[ys, xm, pl.ds(0, mid)], rb.at[ys, xm, pl.ds(0, mid)], ags, 5, right)
    b_l.wait_recv()
    b_l2 = send(rb.at[ys, xp, pl.ds(mid, mid)], rb.at[ys, xp, pl.ds(mid, mid)], ags, 6, left)
    b_r2.wait_recv()
    b_l2.wait_recv()
    b_y = send(rb.at[ys], rb.at[ys], ags, 7, pair)
    a_r.wait_recv()
    a_r2 = send(ra.at[0, xm], ra.at[0, xm], ags, 8, right)
    a_l.wait_recv()
    a_l2 = send(ra.at[1, xp], ra.at[1, xp], ags, 9, left)
    w_d = []
    for i in range(3):
        w_y[i].wait_recv()
        w_d.append(send(part(stores[i], 1), part(stores[i], 3), ws, 6 + i, core))
    a_r2.wait_recv()
    a_l2.wait_recv()
    b_y.wait_recv()
    for i in range(3):
        w_c[i].wait_recv()
        w_d[i].wait_recv()
        w_l[i].wait()

    amount = act.shape[0]
    xa = ra[...].reshape(amount, half_cols)
    xb = rb[...].reshape(amount, half_cols)

    def wide(x_half, w_half):
        return lax.dot_general(
            x_half, w_half, (((1,), (1,)), ((), ())), preferred_element_type=F32
        )

    units = act.shape[1]
    step = 256
    for n in range(0, units, step):
        width = min(step, units - n)
        gate_part = wide(xa, wg[n : n + width, :half_cols]) + wide(xb, wg[n : n + width, half_cols:])
        up_part = wide(xa, wu[n : n + width, :half_cols]) + wide(xb, wu[n : n + width, half_cols:])
        act[:, n : n + width] = (
            gate_part / (1.0 + jnp.exp(-gate_part)) * up_part
        ).astype(BF16)
    for n in range(0, half_cols, step):
        for store, base in ((pa, 0), (pb, half_cols)):
            store[:, :, :, n : n + step] = jnp.dot(
                act[...], wd[:, base + n : base + n + step], preferred_element_type=F32
            ).astype(BF16).reshape(2, 4, block, step)

    b1 = send(pb.at[yo], tb1, rss, 0, pair)
    a1r = send(pa.at[0, x2], ta1.at[0], rss, 1, right)
    a1l = send(pa.at[1, x2], ta1.at[1], rss, 2, left)
    a1r.wait_recv()
    pa[0, xp] = (pa[0, xp].astype(F32) + ta1[0].astype(F32)).astype(BF16)
    a2r = send(pa.at[:, xp], ta2.at[0], rss, 3, right)
    a1l.wait_recv()
    pa[1, xm] = (pa[1, xm].astype(F32) + ta1[1].astype(F32)).astype(BF16)
    a2l = send(pa.at[:, xm], ta2.at[1], rss, 4, left)
    b1.wait_recv()
    pb[ys, x2] = (pb[ys, x2].astype(F32) + tb1[x2].astype(F32)).astype(BF16)
    b2r = send(pb.at[ys, x2, pl.ds(0, mid)], tb2.at[0], rss, 5, right)
    b2l = send(pb.at[ys, x2, pl.ds(mid, mid)], tb2.at[1], rss, 6, left)
    for spot in (xp, xm):
        pb[ys, spot] = (pb[ys, spot].astype(F32) + tb1[spot].astype(F32)).astype(BF16)
    a2r.wait_recv()
    a2l.wait_recv()
    for k in range(2):
        sa[k] = (
            pa[k, x].astype(F32) + ta2[0, k].astype(F32) + ta2[1, k].astype(F32)
        ).astype(BF16)
    a3 = send(sa.at[yo], ta3, rss, 7, pair)
    b2r.wait_recv()
    pb[ys, xp, 0:mid] = (pb[ys, xp, 0:mid].astype(F32) + tb2[0].astype(F32)).astype(BF16)
    b3r = send(pb.at[ys, xp], tb3.at[0], rss, 8, right)
    b2l.wait_recv()
    pb[ys, xm, mid:block] = (pb[ys, xm, mid:block].astype(F32) + tb2[1].astype(F32)).astype(BF16)
    b3l = send(pb.at[ys, xm], tb3.at[1], rss, 9, left)
    own_b = pb[ys, x].astype(F32) + tb1[x].astype(F32)
    a3.wait_recv()
    final_a = sa[ys].astype(F32) + ta3[...].astype(F32)
    b3r.wait_recv()
    b3l.wait_recv()
    final_b = own_b + tb3[0].astype(F32) + tb3[1].astype(F32)

    for d in range(nz):
        ret_out[d, :, :half_cols] = final_a[d * cap : (d + 1) * cap].astype(BF16)
        ret_out[d, :, half_cols:] = final_b[d * cap : (d + 1) * cap].astype(BF16)
    home = [
        send(ret_out.at[d], ret_in.at[d - 1], zs, 13 + d, behind(d)) for d in (4, 3, 5, 2, 6, 1, 7)
    ]
    weights = jnp.where(named[0], egate[:, 0:1], 0.0) + jnp.where(named[1], egate[:, 1:2], 0.0)
    weights = placing * weights
    high = weights.astype(BF16)
    low = (weights - high.astype(F32)).astype(BF16)
    both = jnp.concatenate([high, low], axis=0)
    for copy in home:
        copy.wait_recv()
    back = jnp.concatenate(
        [ret_out[0].astype(F32)] + [ret_in[d].astype(F32) for d in range(nz - 1)], axis=0
    ).astype(BF16)
    mixed = jnp.dot(both, back, preferred_element_type=F32)
    mix_ref[...] = (mixed[:rows] + mixed[rows:]).astype(BF16)
    for copy in started:
        copy.wait_send()


def moe_layer(partial, residual, gain, route, egate, g_t, u_t, down):
    nz, rows, width = partial.shape
    half_cols = width // 2
    hidden = g_t.shape[0]
    cap = max(2, 2 * TOPA * rows // nz)
    block = nz * cap
    amount = 8 * block
    units = 4 * hidden
    vmem = pl.BlockSpec(memory_space=pltpu.VMEM)
    hbm = pl.BlockSpec(memory_space=pl.ANY)

    def buf(*shape):
        return pltpu.VMEM(shape, BF16)

    def dma(n):
        return pltpu.SemaphoreType.DMA((n,))

    return pl.pallas_call(
        layer_kernel,
        out_shape=(
            jax.ShapeDtypeStruct((rows, width), BF16),
            jax.ShapeDtypeStruct((rows, width), BF16),
        ),
        in_specs=[vmem] * 5 + [hbm] * 3,
        out_specs=(vmem, vmem),
        scratch_shapes=[
            buf(nz - 1, rows, width),
            buf(nz, cap, width),
            buf(nz - 1, cap, width),
            buf(2, 4, block, half_cols),
            buf(2, 4, block, half_cols),
            buf(units, width),
            buf(units, width),
            buf(units, width),
            buf(amount, units),
            buf(2, 4, block, half_cols),
            buf(2, 4, block, half_cols),
            buf(2, block, half_cols),
            buf(2, 2, block, half_cols),
            buf(2, block, half_cols),
            buf(block, half_cols),
            buf(4, block, half_cols),
            buf(2, block // 2, half_cols),
            buf(2, block, half_cols),
            buf(nz, cap, width),
            buf(nz - 1, cap, width),
            dma(3 * (nz - 1)), dma(3 * (nz - 1)),
            dma(10), dma(10), dma(10), dma(10), dma(9), dma(9), dma(3),
        ],
        compiler_params=pltpu.CompilerParams(
            collective_id=0, has_side_effects=True, vmem_limit_bytes=VMEM_LIMIT
        ),
        name="moe_layer",
    )(partial, residual, gain, route, egate, g_t, u_t, down)


def local(
    residual, queries, kv_cache, page_table, seq_lengths, head_route, head_gate, out_weight,
    norm_gain, expert_route, expert_gate, gate_up, down_weight,
):
    turned = jnp.transpose(gate_up[0], (0, 2, 1))
    partial = attention(
        page_table, seq_lengths, jnp.transpose(queries, (1, 0, 2)), head_route, head_gate,
        kv_cache, out_weight,
    )
    rows, width = residual.shape
    return moe_layer(
        partial.reshape(-1, rows, width), residual, norm_gain.reshape(1, -1), expert_route,
        expert_gate, turned[0], turned[1], down_weight[0],
    )


def solution(mesh):
    return jax.shard_map(
        local,
        mesh=mesh,
        in_specs=(
            P(("req", "exp"), None),
            P("req", None, "exp"),
            P("req", None, None, "exp"),
            P("req", None),
            P("req"),
            P("req", None),
            P("req", None),
            P(None, "exp", None),
            P(),
            P(("req", "exp"), None),
            P(("req", "exp"), None),
            P("exp", None, None, "req"),
            P("exp", "req", None),
        ),
        out_specs=(P(("req", "exp"), None), P(("req", "exp"), None)),
        check_vma=False,
    )
```

```python
import jax
import jax.numpy as jnp
from jax import lax
from jax.experimental import pallas as pl
from jax.experimental.pallas import tpu as pltpu
from jax.sharding import PartitionSpec as P

HD = 128
TOPA = 2
SPAN = 120
F32 = jnp.float32
BF16 = jnp.bfloat16
MESH = pl.DeviceIdType.MESH
VMEM_LIMIT = 60 * 1024 * 1024


def column(row):
    n = row.shape[1]
    same = lax.broadcasted_iota(jnp.int32, (n, n), 0) == lax.broadcasted_iota(jnp.int32, (n, n), 1)
    return jnp.sum(jnp.where(same, jnp.broadcast_to(row, (n, n)), 0.0), axis=1, keepdims=True)


def attend(q, k, v, allowed):
    scores = lax.dot_general(
        q, k, (((1,), (1,)), ((), ())), preferred_element_type=F32
    ) * HD ** (-0.5)
    scores = jnp.where(allowed, scores, -1e30)
    raised = jnp.exp(scores - jnp.max(scores, axis=1, keepdims=True))
    total = jnp.sum(raised, axis=1, keepdims=True)
    return jnp.dot(raised.astype(BF16), v, preferred_element_type=F32) / total


def layer_kernel(
    table, lengths, q_ref, head_route, head_gate, residual, gain, route, egate,
    kv_hbm, w_hbm, gu_hbm, d_hbm, attended_ref, mix_ref,
    kv, w, mix, x_rows, partial, rs_buf, out_buf, in_buf, ra, rb, wg, wu, wd, act, pa, pb,
    ta1, ta2, sa, ta3, tb1, tb2, tb3, ret_out, ret_in,
    kv_sem, o_sem, s_send, s_recv, z_send, z_recv, ag_send, ag_recv, rs_send, rs_recv,
    w_send, w_recv, l_sem,
):
    nz = partial.shape[0]
    rows = residual.shape[0]
    cap = out_buf.shape[1]
    block = nz * cap
    half_cols = ra.shape[3]
    hidden = d_hbm.shape[0]
    me = lax.axis_index("req")
    z = lax.axis_index("exp")
    c = lax.rem(me, 2)
    y = lax.rem(lax.div(me, 2), 4)
    x = lax.div(me, 8)
    xp, xm, x2 = lax.rem(x + 1, 4), lax.rem(x + 3, 4), lax.rem(x + 2, 4)
    yw = y + 1 - 2 * lax.rem(y, 2)
    turned = lax.rem(y + 3, 4)
    ys = lax.rem(turned, 2)
    yo = 1 - ys
    yr = lax.rem(turned + 1 - 2 * ys + 1, 4)

    def dev(x_, y_, c_):
        return ((x_ * 4 + y_) * 2 + c_, z)

    right, left = dev(xp, y, c), dev(xm, y, c)
    pair = dev(x, yr, c)
    w_pair = dev(x, yw, c)
    core = dev(x, y, 1 - c)

    def ahead(d):
        return (me, lax.rem(z + d, nz))

    def behind(d):
        return (me, lax.rem(z + nz - d, nz))

    barrier = pltpu.get_barrier_semaphore()
    others = [ahead(d) for d in range(1, nz)] + [right, left, pair, w_pair, core]
    for other in others:
        pl.semaphore_signal(barrier, inc=1, device_id=other, device_id_type=MESH)
    kv_copy = pltpu.make_async_copy(kv_hbm, kv, kv_sem.at[0])
    kv_copy.start()
    experts = w.shape[0]
    o_copies = [pltpu.make_async_copy(w_hbm.at[e], w.at[e], o_sem.at[e]) for e in range(experts)]
    for copy in o_copies:
        copy.start()
    pl.semaphore_wait(barrier, len(others))

    started = []

    def send(src, dst, sems, i, device):
        copy = pltpu.make_async_remote_copy(
            src_ref=src, dst_ref=dst, send_sem=sems[0].at[i], recv_sem=sems[1].at[i],
            device_id=device, device_id_type=MESH,
        )
        copy.start()
        started.append(copy)
        return copy

    zs, ags, rss, ws = (z_send, z_recv), (ag_send, ag_recv), (rs_send, rs_recv), (w_send, w_recv)
    ss = (s_send, s_recv)
    far_first = (4, 3, 5, 2, 6, 1, 7)

    sources, stores = (gu_hbm.at[0], gu_hbm.at[1], d_hbm), (wg, wu, wd)

    def part(store, b):
        return store.at[pl.ds(b * hidden, hidden)]

    w_y = [send(sources[i], part(stores[i], 1), ws, i, w_pair) for i in range(3)]
    w_c = [send(sources[i], part(stores[i], 2), ws, 3 + i, core) for i in range(3)]
    w_l = [
        pltpu.make_async_copy(sources[i], part(stores[i], 0), l_sem.at[i]) for i in range(3)
    ]
    for copy in w_l:
        copy.start()

    pages = table.shape[1]
    decodes = table.shape[0] - 1
    page = kv.shape[2]
    width = q_ref.shape[2]
    tokens = q_ref.shape[1]
    keys = pages * page
    row_pos = lengths[0] - SPAN + lax.broadcasted_iota(jnp.int32, (tokens, keys), 0)
    causal = lax.broadcasted_iota(jnp.int32, (tokens, keys), 1) <= row_pos
    tail = 2 * decodes
    d_keys = decodes * page
    d_row = lax.broadcasted_iota(jnp.int32, (TOPA * tail, d_keys), 0) % tail - decodes
    d_col = lax.broadcasted_iota(jnp.int32, (TOPA * tail, d_keys), 1)
    d_slot = d_col // page
    length_of = jnp.zeros((TOPA * tail, d_keys), jnp.int32)
    for s in range(decodes):
        length_of = jnp.where(d_slot == s, lengths[s + 1], length_of)
    d_allowed = (d_slot == d_row) & (d_col % page < length_of)
    kv_copy.wait()
    for h in range(width // HD):
        cols = slice(h * HD, (h + 1) * HD)

        def paged(kind, spots):
            return jnp.concatenate([kv[table[s, p], kind, :, cols] for s, p in spots], axis=0)

        pre = [(0, p) for p in range(pages)]
        k_pre, v_pre = paged(0, pre), paged(1, pre)
        for t in range(TOPA):
            mix[t, :, cols] = attend(q_ref[t, :, cols], k_pre, v_pre, causal)
        dec = [(s + 1, 0) for s in range(decodes)]
        k_dec, v_dec = paged(0, dec), paged(1, dec)
        q_dec = jnp.concatenate(
            [q_ref[t, tokens - tail : tokens, cols] for t in range(TOPA)], axis=0
        )
        o_dec = attend(q_dec, k_dec, v_dec, d_allowed)
        for t in range(TOPA):
            mix[t, SPAN:tokens, cols] = o_dec[t * tail + decodes : (t + 1) * tail]
    mixes = [mix[t].astype(BF16).astype(F32) for t in range(TOPA)]
    routes = [column(head_route[t : t + 1].astype(F32)) for t in range(TOPA)]
    gates = [column(head_gate[t : t + 1]) for t in range(TOPA)]
    for e in range(experts):
        gated = jnp.zeros((tokens, width), F32)
        for t in range(TOPA):
            gated = gated + jnp.where(routes[t] == e, gates[t], 0.0) * mixes[t]
        x_rows[:, e * width : (e + 1) * width] = gated.astype(BF16)
    for copy in o_copies:
        copy.wait()

    outs = w.shape[2]
    chunk = outs // 4
    scatter = []
    for n in range(0, outs, chunk):
        partial[:, :, n : n + chunk] = jnp.dot(
            x_rows[...],
            w[:, :, n : n + chunk].reshape(experts * width, chunk),
            preferred_element_type=F32,
        ).astype(BF16).reshape(nz, rows, chunk)
        for d in far_first:
            scatter.append(
                send(
                    partial.at[lax.rem(z + d, nz), :, pl.ds(n, chunk)],
                    rs_buf.at[d - 1, :, pl.ds(n, chunk)],
                    ss, (n // chunk) * (nz - 1) + d - 1, ahead(d),
                )
            )

    def routed(t):
        rel = column(route[t : t + 1].astype(F32)) - z.astype(F32)
        rel = jnp.where(rel < 0, rel + nz, rel)
        spot = lax.broadcasted_iota(jnp.int32, (rows, block), 1) // cap
        return rel == spot.astype(F32)

    named = [routed(t) for t in range(TOPA)]
    member = jnp.where(named[0] | named[1], 1.0, 0.0).astype(F32)
    lower = jnp.where(
        lax.broadcasted_iota(jnp.int32, (rows, rows), 1)
        < lax.broadcasted_iota(jnp.int32, (rows, rows), 0),
        1.0, 0.0,
    ).astype(BF16)
    rank = jnp.dot(lower, member.astype(BF16), preferred_element_type=F32)
    place = (lax.broadcasted_iota(jnp.int32, (rows, block), 1) % cap).astype(F32)
    placing = jnp.where(rank == place, member, 0.0)
    egates = [column(egate[t : t + 1]) for t in range(TOPA)]

    for copy in scatter:
        copy.wait_recv()
    summed = residual[...].astype(F32) + partial[z].astype(F32)
    for d in range(nz - 1):
        summed = summed + rs_buf[d].astype(F32)
    attended = summed.astype(BF16)
    attended_ref[...] = attended
    values = attended.astype(F32)
    normed = (
        values
        * lax.rsqrt(jnp.mean(values * values, axis=1, keepdims=True) + 1e-06)
        * gain[...]
    ).astype(BF16)
    outgoing = lax.dot_general(
        placing.astype(BF16), normed, (((0,), (0,)), ((), ())), preferred_element_type=F32
    )
    for d in range(nz):
        out_buf[d] = outgoing[d * cap : (d + 1) * cap].astype(BF16)
    dispatch = [
        send(out_buf.at[d], in_buf.at[d - 1], zs, d - 1, ahead(d)) for d in far_first
    ]
    for copy in dispatch:
        copy.wait_recv()
    arrived = jnp.concatenate(
        [out_buf[0].astype(F32)] + [in_buf[d].astype(F32) for d in range(nz - 1)], axis=0
    ).astype(BF16)

    ra[ys, x] = arrived[:, :half_cols]
    rb[ys, x] = arrived[:, half_cols:]
    mid = block // 2
    a_y = send(ra.at[ys, x], ra.at[ys, x], ags, 0, pair)
    b_r = send(rb.at[ys, x], rb.at[ys, x], ags, 1, right)
    b_l = send(rb.at[ys, x], rb.at[ys, x], ags, 2, left)
    a_y.wait_recv()
    a_r = send(ra.at[:, x], ra.at[:, x], ags, 3, right)
    a_l = send(ra.at[:, x], ra.at[:, x], ags, 4, left)
    b_r.wait_recv()
    b_r2 = send(rb.at[ys, xm, pl.ds(0, mid)], rb.at[ys, xm, pl.ds(0, mid)], ags, 5, right)
    b_l.wait_recv()
    b_l2 = send(rb.at[ys, xp, pl.ds(mid, mid)], rb.at[ys, xp, pl.ds(mid, mid)], ags, 6, left)
    b_r2.wait_recv()
    b_l2.wait_recv()
    b_y = send(rb.at[ys], rb.at[ys], ags, 7, pair)
    a_r.wait_recv()
    a_r2 = send(ra.at[0, xm], ra.at[0, xm], ags, 8, right)
    a_l.wait_recv()
    a_l2 = send(ra.at[1, xp], ra.at[1, xp], ags, 9, left)
    w_d = []
    for i in range(2):
        w_y[i].wait_recv()
        w_d.append(send(part(stores[i], 1), part(stores[i], 3), ws, 6 + i, core))
    a_r2.wait_recv()
    a_l2.wait_recv()
    b_y.wait_recv()
    for i in range(2):
        w_c[i].wait_recv()
        w_d[i].wait_recv()
        w_l[i].wait()

    amount = act.shape[0]
    xa = ra[...].reshape(amount, half_cols)
    xb = rb[...].reshape(amount, half_cols)

    def wide(x_half, w_half):
        return lax.dot_general(
            x_half, w_half, (((1,), (1,)), ((), ())), preferred_element_type=F32
        )

    units = act.shape[1]
    step = 256
    for n in range(0, units, step):
        size = min(step, units - n)
        gate_part = wide(xa, wg[n : n + size, :half_cols]) + wide(xb, wg[n : n + size, half_cols:])
        up_part = wide(xa, wu[n : n + size, :half_cols]) + wide(xb, wu[n : n + size, half_cols:])
        act[:, n : n + size] = (
            gate_part / (1.0 + jnp.exp(-gate_part)) * up_part
        ).astype(BF16)
    w_y[2].wait_recv()
    w_d.append(send(part(wd, 1), part(wd, 3), ws, 8, core))
    w_c[2].wait_recv()
    w_l[2].wait()
    w_d[2].wait_recv()
    for n in range(0, half_cols, step):
        for store, base in ((pa, 0), (pb, half_cols)):
            store[:, :, :, n : n + step] = jnp.dot(
                act[...], wd[:, base + n : base + n + step], preferred_element_type=F32
            ).astype(BF16).reshape(2, 4, block, step)

    b1 = send(pb.at[yo], tb1, rss, 0, pair)
    a1r = send(pa.at[0, x2], ta1.at[0], rss, 1, right)
    a1l = send(pa.at[1, x2], ta1.at[1], rss, 2, left)
    a1r.wait_recv()
    pa[0, xp] = (pa[0, xp].astype(F32) + ta1[0].astype(F32)).astype(BF16)
    a2r = send(pa.at[:, xp], ta2.at[0], rss, 3, right)
    a1l.wait_recv()
    pa[1, xm] = (pa[1, xm].astype(F32) + ta1[1].astype(F32)).astype(BF16)
    a2l = send(pa.at[:, xm], ta2.at[1], rss, 4, left)
    b1.wait_recv()
    pb[ys, x2] = (pb[ys, x2].astype(F32) + tb1[x2].astype(F32)).astype(BF16)
    b2r = send(pb.at[ys, x2, pl.ds(0, mid)], tb2.at[0], rss, 5, right)
    b2l = send(pb.at[ys, x2, pl.ds(mid, mid)], tb2.at[1], rss, 6, left)
    for spot in (xp, xm):
        pb[ys, spot] = (pb[ys, spot].astype(F32) + tb1[spot].astype(F32)).astype(BF16)
    a2r.wait_recv()
    a2l.wait_recv()
    for k in range(2):
        sa[k] = (
            pa[k, x].astype(F32) + ta2[0, k].astype(F32) + ta2[1, k].astype(F32)
        ).astype(BF16)
    a3 = send(sa.at[yo], ta3, rss, 7, pair)
    b2r.wait_recv()
    pb[ys, xp, 0:mid] = (pb[ys, xp, 0:mid].astype(F32) + tb2[0].astype(F32)).astype(BF16)
    b3r = send(pb.at[ys, xp], tb3.at[0], rss, 8, right)
    b2l.wait_recv()
    pb[ys, xm, mid:block] = (pb[ys, xm, mid:block].astype(F32) + tb2[1].astype(F32)).astype(BF16)
    b3l = send(pb.at[ys, xm], tb3.at[1], rss, 9, left)
    own_b = pb[ys, x].astype(F32) + tb1[x].astype(F32)
    a3.wait_recv()
    final_a = sa[ys].astype(F32) + ta3[...].astype(F32)
    b3r.wait_recv()
    b3l.wait_recv()
    final_b = own_b + tb3[0].astype(F32) + tb3[1].astype(F32)

    for d in range(nz):
        ret_out[d, :, :half_cols] = final_a[d * cap : (d + 1) * cap].astype(BF16)
        ret_out[d, :, half_cols:] = final_b[d * cap : (d + 1) * cap].astype(BF16)
    home = [
        send(ret_out.at[d], ret_in.at[d - 1], zs, nz - 2 + d, behind(d)) for d in far_first
    ]
    weights = jnp.where(named[0], egates[0], 0.0) + jnp.where(named[1], egates[1], 0.0)
    weights = placing * weights
    high = weights.astype(BF16)
    low = (weights - high.astype(F32)).astype(BF16)
    both = jnp.concatenate([high, low], axis=0)
    for copy in home:
        copy.wait_recv()
    back = jnp.concatenate(
        [ret_out[0].astype(F32)] + [ret_in[d].astype(F32) for d in range(nz - 1)], axis=0
    ).astype(BF16)
    mixed = jnp.dot(both, back, preferred_element_type=F32)
    mix_ref[...] = (mixed[:rows] + mixed[rows:]).astype(BF16)
    for copy in started:
        copy.wait_send()


def layer(
    table, lengths, q, head_route, head_gate, residual, gain, route, egate,
    kv_cache, out_weight, gate_up, down,
):
    pool, _, page, head_width = kv_cache.shape
    experts = out_weight.shape[0]
    tokens = q.shape[1]
    rows, width = residual.shape
    nz = tokens // rows
    half_cols = width // 2
    hidden = down.shape[0]
    cap = max(2, 2 * TOPA * rows // nz)
    block = nz * cap
    amount = 8 * block
    units = 4 * hidden
    vmem = pl.BlockSpec(memory_space=pltpu.VMEM)
    smem = pl.BlockSpec(memory_space=pltpu.SMEM)
    hbm = pl.BlockSpec(memory_space=pl.ANY)

    def buf(*shape):
        return pltpu.VMEM(shape, BF16)

    def dma(n):
        return pltpu.SemaphoreType.DMA((n,))

    return pl.pallas_call(
        layer_kernel,
        out_shape=(
            jax.ShapeDtypeStruct((rows, width), BF16),
            jax.ShapeDtypeStruct((rows, width), BF16),
        ),
        in_specs=[smem] * 2 + [vmem] * 7 + [hbm] * 4,
        out_specs=(vmem, vmem),
        scratch_shapes=[
            buf(pool, 2, page, head_width),
            buf(experts, head_width, width),
            pltpu.VMEM((TOPA, tokens, head_width), F32),
            buf(tokens, experts * head_width),
            buf(nz, rows, width),
            buf(nz - 1, rows, width),
            buf(nz, cap, width),
            buf(nz - 1, cap, width),
            buf(2, 4, block, half_cols),
            buf(2, 4, block, half_cols),
            buf(units, width),
            buf(units, width),
            buf(units, width),
            buf(amount, units),
            buf(2, 4, block, half_cols),
            buf(2, 4, block, half_cols),
            buf(2, block, half_cols),
            buf(2, 2, block, half_cols),
            buf(2, block, half_cols),
            buf(block, half_cols),
            buf(4, block, half_cols),
            buf(2, block // 2, half_cols),
            buf(2, block, half_cols),
            buf(nz, cap, width),
            buf(nz - 1, cap, width),
            dma(1), dma(experts),
            dma(4 * (nz - 1)), dma(4 * (nz - 1)), dma(2 * (nz - 1)), dma(2 * (nz - 1)),
            dma(10), dma(10), dma(10), dma(10), dma(9), dma(9), dma(3),
        ],
        compiler_params=pltpu.CompilerParams(
            collective_id=0, has_side_effects=True, vmem_limit_bytes=VMEM_LIMIT
        ),
        name="layer",
    )(
        table, lengths, q, head_route, head_gate, residual, gain, route, egate,
        kv_cache, out_weight, gate_up, down,
    )


def local(
    residual, queries, kv_cache, page_table, seq_lengths, head_route, head_gate, out_weight,
    norm_gain, expert_route, expert_gate, gate_up, down_weight,
):
    return layer(
        page_table, seq_lengths, jnp.transpose(queries, (1, 0, 2)), head_route.T, head_gate.T,
        residual, norm_gain.reshape(1, -1), expert_route.T, expert_gate.T,
        kv_cache, out_weight, jnp.transpose(gate_up[0], (0, 2, 1)), down_weight[0],
    )


def solution(mesh):
    return jax.shard_map(
        local,
        mesh=mesh,
        in_specs=(
            P(("req", "exp"), None),
            P("req", None, "exp"),
            P("req", None, None, "exp"),
            P("req", None),
            P("req"),
            P("req", None),
            P("req", None),
            P(None, "exp", None),
            P(),
            P(("req", "exp"), None),
            P(("req", "exp"), None),
            P("exp", None, None, "req"),
            P("exp", "req", None),
        ),
        out_specs=(P(("req", "exp"), None), P(("req", "exp"), None)),
        check_vma=False,
    )
```

```python
import jax
import jax.numpy as jnp
from jax import lax
from jax.experimental import pallas as pl
from jax.experimental.pallas import tpu as pltpu
from jax.sharding import PartitionSpec as P

HD = 128
TOPA = 2
SPAN = 120
F32 = jnp.float32
BF16 = jnp.bfloat16
MESH = pl.DeviceIdType.MESH
VMEM_LIMIT = 60 * 1024 * 1024


def column(row):
    n = row.shape[1]
    same = lax.broadcasted_iota(jnp.int32, (n, n), 0) == lax.broadcasted_iota(jnp.int32, (n, n), 1)
    return jnp.sum(jnp.where(same, jnp.broadcast_to(row, (n, n)), 0.0), axis=1, keepdims=True)


def attend(q, k, v, allowed):
    scores = lax.dot_general(
        q, k, (((1,), (1,)), ((), ())), preferred_element_type=F32
    ) * HD ** (-0.5)
    scores = jnp.where(allowed, scores, -1e30)
    raised = jnp.exp(scores - jnp.max(scores, axis=1, keepdims=True))
    total = jnp.sum(raised, axis=1, keepdims=True)
    return jnp.dot(raised.astype(BF16), v, preferred_element_type=F32) / total


def layer_kernel(
    table, lengths, q_ref, head_route, head_gate, residual, gain, route, egate,
    kv_hbm, w_hbm, gu_hbm, d_hbm, attended_ref, mix_ref,
    kv, w, mix, x_rows, partial, rs_buf, out_buf, in_buf, ra, rb, wg, wu, wd, act, pa, pb,
    ta1, ta2, sa, ta3, tb1, tb2, tb3, ret_out, ret_in,
    kv_sem, o_sem, s_send, s_recv, z_send, z_recv, ag_send, ag_recv, rs_send, rs_recv,
    w_send, w_recv, l_sem,
):
    nz = partial.shape[0]
    rows = residual.shape[0]
    cap = out_buf.shape[1]
    block = nz * cap
    half_cols = ra.shape[3]
    hidden = d_hbm.shape[0]
    me = lax.axis_index("req")
    z = lax.axis_index("exp")
    c = lax.rem(me, 2)
    y = lax.rem(lax.div(me, 2), 4)
    x = lax.div(me, 8)
    xp, xm, x2 = lax.rem(x + 1, 4), lax.rem(x + 3, 4), lax.rem(x + 2, 4)
    yw = y + 1 - 2 * lax.rem(y, 2)
    turned = lax.rem(y + 3, 4)
    ys = lax.rem(turned, 2)
    yo = 1 - ys
    yr = lax.rem(turned + 1 - 2 * ys + 1, 4)

    def dev(x_, y_, c_):
        return ((x_ * 4 + y_) * 2 + c_, z)

    right, left = dev(xp, y, c), dev(xm, y, c)
    pair = dev(x, yr, c)
    w_pair = dev(x, yw, c)
    core = dev(x, y, 1 - c)

    def ahead(d):
        return (me, lax.rem(z + d, nz))

    def behind(d):
        return (me, lax.rem(z + nz - d, nz))

    barrier = pltpu.get_barrier_semaphore()
    others = [ahead(d) for d in range(1, nz)] + [right, left, pair, w_pair, core]
    for other in others:
        pl.semaphore_signal(barrier, inc=1, device_id=other, device_id_type=MESH)
    kv_copy = pltpu.make_async_copy(kv_hbm, kv, kv_sem.at[0])
    kv_copy.start()
    experts = w.shape[0]
    o_copies = [pltpu.make_async_copy(w_hbm.at[e], w.at[e], o_sem.at[e]) for e in range(experts)]
    for copy in o_copies:
        copy.start()
    pl.semaphore_wait(barrier, len(others))

    started = []

    def send(src, dst, sems, i, device):
        copy = pltpu.make_async_remote_copy(
            src_ref=src, dst_ref=dst, send_sem=sems[0].at[i], recv_sem=sems[1].at[i],
            device_id=device, device_id_type=MESH,
        )
        copy.start()
        started.append(copy)
        return copy

    zs, ags, rss, ws = (z_send, z_recv), (ag_send, ag_recv), (rs_send, rs_recv), (w_send, w_recv)
    ss = (s_send, s_recv)
    far_first = (4, 3, 5, 2, 6, 1, 7)

    sources, stores = (gu_hbm.at[0], gu_hbm.at[1], d_hbm), (wg, wu, wd)

    def part(store, b):
        return store.at[pl.ds(b * hidden, hidden)]

    w_y = [send(sources[i], part(stores[i], 1), ws, i, w_pair) for i in range(3)]
    w_c = [send(sources[i], part(stores[i], 2), ws, 3 + i, core) for i in range(3)]
    w_l = [
        pltpu.make_async_copy(sources[i], part(stores[i], 0), l_sem.at[i]) for i in range(3)
    ]
    for copy in w_l:
        copy.start()

    pages = table.shape[1]
    decodes = table.shape[0] - 1
    page = kv.shape[2]
    width = q_ref.shape[2]
    tokens = q_ref.shape[1]
    keys = pages * page
    row_pos = lengths[0] - SPAN + lax.broadcasted_iota(jnp.int32, (tokens, keys), 0)
    causal = lax.broadcasted_iota(jnp.int32, (tokens, keys), 1) <= row_pos
    tail = 2 * decodes
    d_keys = decodes * page
    d_row = lax.broadcasted_iota(jnp.int32, (TOPA * tail, d_keys), 0) % tail - decodes
    d_col = lax.broadcasted_iota(jnp.int32, (TOPA * tail, d_keys), 1)
    d_slot = d_col // page
    length_of = jnp.zeros((TOPA * tail, d_keys), jnp.int32)
    for s in range(decodes):
        length_of = jnp.where(d_slot == s, lengths[s + 1], length_of)
    d_allowed = (d_slot == d_row) & (d_col % page < length_of)
    kv_copy.wait()
    for h in range(width // HD):
        cols = slice(h * HD, (h + 1) * HD)

        def paged(kind, spots):
            return jnp.concatenate([kv[table[s, p], kind, :, cols] for s, p in spots], axis=0)

        pre = [(0, p) for p in range(pages)]
        k_pre, v_pre = paged(0, pre), paged(1, pre)
        for t in range(TOPA):
            mix[t, :, cols] = attend(q_ref[t, :, cols], k_pre, v_pre, causal)
        dec = [(s + 1, 0) for s in range(decodes)]
        k_dec, v_dec = paged(0, dec), paged(1, dec)
        q_dec = jnp.concatenate(
            [q_ref[t, tokens - tail : tokens, cols] for t in range(TOPA)], axis=0
        )
        o_dec = attend(q_dec, k_dec, v_dec, d_allowed)
        for t in range(TOPA):
            mix[t, SPAN:tokens, cols] = o_dec[t * tail + decodes : (t + 1) * tail]
    mixes = [mix[t].astype(BF16).astype(F32) for t in range(TOPA)]
    routes = [column(head_route[t : t + 1].astype(F32)) for t in range(TOPA)]
    gates = [column(head_gate[t : t + 1]) for t in range(TOPA)]
    for e in range(experts):
        gated = jnp.zeros((tokens, width), F32)
        for t in range(TOPA):
            gated = gated + jnp.where(routes[t] == e, gates[t], 0.0) * mixes[t]
        x_rows[:, e * width : (e + 1) * width] = gated.astype(BF16)
    for copy in o_copies:
        copy.wait()

    outs = w.shape[2]
    chunk = outs // 4
    scatter = []
    for n in range(0, outs, chunk):
        partial[:, :, n : n + chunk] = jnp.dot(
            x_rows[...],
            w[:, :, n : n + chunk].reshape(experts * width, chunk),
            preferred_element_type=F32,
        ).astype(BF16).reshape(nz, rows, chunk)
        for d in far_first:
            scatter.append(
                send(
                    partial.at[lax.rem(z + d, nz), :, pl.ds(n, chunk)],
                    rs_buf.at[d - 1, :, pl.ds(n, chunk)],
                    ss, (n // chunk) * (nz - 1) + d - 1, ahead(d),
                )
            )

    def routed(t):
        rel = column(route[t : t + 1].astype(F32)) - z.astype(F32)
        rel = jnp.where(rel < 0, rel + nz, rel)
        spot = lax.broadcasted_iota(jnp.int32, (rows, block), 1) // cap
        return rel == spot.astype(F32)

    named = [routed(t) for t in range(TOPA)]
    member = jnp.where(named[0] | named[1], 1.0, 0.0).astype(F32)
    lower = jnp.where(
        lax.broadcasted_iota(jnp.int32, (rows, rows), 1)
        < lax.broadcasted_iota(jnp.int32, (rows, rows), 0),
        1.0, 0.0,
    ).astype(BF16)
    rank = jnp.dot(lower, member.astype(BF16), preferred_element_type=F32)
    place = (lax.broadcasted_iota(jnp.int32, (rows, block), 1) % cap).astype(F32)
    placing = jnp.where(rank == place, member, 0.0)
    egates = [column(egate[t : t + 1]) for t in range(TOPA)]

    for copy in scatter:
        copy.wait_recv()
    summed = residual[...].astype(F32) + partial[z].astype(F32)
    for d in range(nz - 1):
        summed = summed + rs_buf[d].astype(F32)
    attended = summed.astype(BF16)
    attended_ref[...] = attended
    values = attended.astype(F32)
    normed = (
        values
        * lax.rsqrt(jnp.mean(values * values, axis=1, keepdims=True) + 1e-06)
        * gain[...]
    ).astype(BF16)
    outgoing = lax.dot_general(
        placing.astype(BF16), normed, (((0,), (0,)), ((), ())), preferred_element_type=F32
    )
    for d in range(nz):
        out_buf[d] = outgoing[d * cap : (d + 1) * cap].astype(BF16)
    dispatch = [
        send(out_buf.at[d], in_buf.at[d - 1], zs, d - 1, ahead(d)) for d in far_first
    ]
    for copy in dispatch:
        copy.wait_recv()
    arrived = jnp.concatenate(
        [out_buf[0].astype(F32)] + [in_buf[d].astype(F32) for d in range(nz - 1)], axis=0
    ).astype(BF16)

    ra[ys, x] = arrived[:, :half_cols]
    rb[ys, x] = arrived[:, half_cols:]
    mid = block // 2
    low_rows, high_rows = pl.ds(0, mid), pl.ds(mid, mid)

    def forward(buffer, i, device, *spot):
        return send(buffer.at[spot], buffer.at[spot], ags, i, device)

    a_y = forward(ra, 0, pair, ys, x)
    b_r = forward(rb, 1, right, ys, x)
    b_l = forward(rb, 2, left, ys, x)
    a_r = forward(ra, 3, right, ys, x)
    a_l = forward(ra, 4, left, ys, x)
    b_y = forward(rb, 5, pair, ys, x)
    w_d = []

    def relay_weights(i):
        w_y[i].wait_recv()
        w_d.append(send(part(stores[i], 1), part(stores[i], 3), ws, 6 + i, core))

    relay_weights(0)
    b_r.wait_recv()
    b_r2 = forward(rb, 6, right, ys, xm, low_rows)
    b_ym = forward(rb, 7, pair, ys, xm)
    b_l.wait_recv()
    b_l2 = forward(rb, 8, left, ys, xp, high_rows)
    b_yp = forward(rb, 9, pair, ys, xp)
    a_y.wait_recv()
    a_or = forward(ra, 10, right, yo, x)
    a_ol = forward(ra, 11, left, yo, x)
    relay_weights(1)
    a_r.wait_recv()
    a_r2 = forward(ra, 12, right, ys, xm, low_rows)
    a_l.wait_recv()
    a_l2 = forward(ra, 13, left, ys, xp, high_rows)
    b_r2.wait_recv()
    b_l2.wait_recv()
    b_y2 = forward(rb, 14, pair, ys, x2)

    units = act.shape[2]
    step = 256

    def wide(x_half, w_half):
        return lax.dot_general(
            x_half, w_half, (((1,), (1,)), ((), ())), preferred_element_type=F32
        )

    def up_project(spot):
        xa = ra[:, spot].reshape(2 * block, half_cols)
        xb = rb[:, spot].reshape(2 * block, half_cols)
        for n in range(0, units, step):
            size = min(step, units - n)
            here = slice(n, n + size)
            gate_part = wide(xa, wg[here, :half_cols]) + wide(xb, wg[here, half_cols:])
            up_part = wide(xa, wu[here, :half_cols]) + wide(xb, wu[here, half_cols:])
            act[spot, :, here] = (
                gate_part / (1.0 + jnp.exp(-gate_part)) * up_part
            ).astype(BF16)

    def down_project(spot):
        for n in range(0, half_cols, 2 * step):
            for store, base in ((pb, half_cols), (pa, 0)):
                store[:, spot, :, n : n + 2 * step] = jnp.dot(
                    act[spot], wd[:, base + n : base + n + 2 * step], preferred_element_type=F32
                ).astype(BF16).reshape(2, block, 2 * step)

    for i in range(2):
        w_c[i].wait_recv()
        w_d[i].wait_recv()
        w_l[i].wait()
    b_y.wait_recv()
    up_project(x)
    a_or.wait_recv()
    a_or2 = forward(ra, 15, right, yo, xm, low_rows)
    a_ol.wait_recv()
    a_ol2 = forward(ra, 16, left, yo, xp, high_rows)
    b_ym.wait_recv()
    up_project(xm)
    relay_weights(2)
    b_yp.wait_recv()
    up_project(xp)
    for copy in (a_r2, a_l2, a_or2, a_ol2, b_y2):
        copy.wait_recv()
    up_project(x2)
    w_c[2].wait_recv()
    w_l[2].wait()
    w_d[2].wait_recv()

    down_project(x2)
    a1r = send(pa.at[yo, x2, low_rows], ta1.at[0, 0], rss, 0, right)
    a1l = send(pa.at[yo, x2, high_rows], ta1.at[0, 1], rss, 1, left)
    b1_2 = send(pb.at[yo, x2], tb1.at[0], rss, 2, pair)
    a1rs = send(pa.at[ys, x2, low_rows], ta1.at[1, 0], rss, 3, right)
    a1ls = send(pa.at[ys, x2, high_rows], ta1.at[1, 1], rss, 4, left)
    down_project(xp)
    b1_p = send(pb.at[yo, xp], tb1.at[1], rss, 5, pair)
    down_project(xm)
    b1_m = send(pb.at[yo, xm], tb1.at[2], rss, 6, pair)

    def add(store, term, *spot):
        store[spot] = (store[spot].astype(F32) + term.astype(F32)).astype(BF16)

    low, high = slice(0, mid), slice(mid, block)
    a1r.wait_recv()
    add(pa, ta1[0, 0], yo, xp, low)
    a2r = send(pa.at[yo, xp], ta2.at[0, 0], rss, 7, right)
    a1l.wait_recv()
    add(pa, ta1[0, 1], yo, xm, high)
    a2l = send(pa.at[yo, xm], ta2.at[0, 1], rss, 8, left)
    b1_2.wait_recv()
    add(pb, tb1[0], ys, x2)
    b2r = send(pb.at[ys, x2, low_rows], tb2.at[0], rss, 9, right)
    b2l = send(pb.at[ys, x2, high_rows], tb2.at[1], rss, 10, left)
    a1rs.wait_recv()
    add(pa, ta1[1, 0], ys, xp, low)
    a2rs = send(pa.at[ys, xp], ta2.at[1, 0], rss, 11, right)
    a1ls.wait_recv()
    add(pa, ta1[1, 1], ys, xm, high)
    a2ls = send(pa.at[ys, xm], ta2.at[1, 1], rss, 12, left)
    down_project(x)
    a2r.wait_recv()
    a2l.wait_recv()
    sa[...] = (
        pa[yo, x].astype(F32) + ta2[0, 0].astype(F32) + ta2[0, 1].astype(F32)
    ).astype(BF16)
    a3 = send(sa, ta3, rss, 13, pair)
    b1_x = send(pb.at[yo, x], tb1.at[3], rss, 14, pair)
    b1_p.wait_recv()
    add(pb, tb1[1], ys, xp)
    b1_m.wait_recv()
    add(pb, tb1[2], ys, xm)
    b2r.wait_recv()
    add(pb, tb2[0], ys, xp, low)
    b3r = send(pb.at[ys, xp], tb3.at[0], rss, 15, right)
    b2l.wait_recv()
    add(pb, tb2[1], ys, xm, high)
    b3l = send(pb.at[ys, xm], tb3.at[1], rss, 16, left)
    a2rs.wait_recv()
    a2ls.wait_recv()
    final_a = pa[ys, x].astype(F32) + ta2[1, 0].astype(F32) + ta2[1, 1].astype(F32)
    a3.wait_recv()
    final_a = final_a + ta3[...].astype(F32)
    b1_x.wait_recv()
    final_b = pb[ys, x].astype(F32) + tb1[3].astype(F32)
    b3r.wait_recv()
    b3l.wait_recv()
    final_b = final_b + tb3[0].astype(F32) + tb3[1].astype(F32)

    for d in range(nz):
        ret_out[d, :, :half_cols] = final_a[d * cap : (d + 1) * cap].astype(BF16)
        ret_out[d, :, half_cols:] = final_b[d * cap : (d + 1) * cap].astype(BF16)
    home = [
        send(ret_out.at[d], ret_in.at[d - 1], zs, nz - 2 + d, behind(d)) for d in far_first
    ]
    weights = jnp.where(named[0], egates[0], 0.0) + jnp.where(named[1], egates[1], 0.0)
    weights = placing * weights
    coarse = weights.astype(BF16)
    fine = (weights - coarse.astype(F32)).astype(BF16)
    both = jnp.concatenate([coarse, fine], axis=0)
    for copy in home:
        copy.wait_recv()
    back = jnp.concatenate(
        [ret_out[0].astype(F32)] + [ret_in[d].astype(F32) for d in range(nz - 1)], axis=0
    ).astype(BF16)
    mixed = jnp.dot(both, back, preferred_element_type=F32)
    mix_ref[...] = (mixed[:rows] + mixed[rows:]).astype(BF16)
    for copy in started:
        copy.wait_send()


def layer(
    table, lengths, q, head_route, head_gate, residual, gain, route, egate,
    kv_cache, out_weight, gate_up, down,
):
    pool, _, page, head_width = kv_cache.shape
    experts = out_weight.shape[0]
    tokens = q.shape[1]
    rows, width = residual.shape
    nz = tokens // rows
    half_cols = width // 2
    hidden = down.shape[0]
    cap = max(2, 2 * TOPA * rows // nz)
    block = nz * cap
    units = 4 * hidden
    vmem = pl.BlockSpec(memory_space=pltpu.VMEM)
    smem = pl.BlockSpec(memory_space=pltpu.SMEM)
    hbm = pl.BlockSpec(memory_space=pl.ANY)

    def buf(*shape):
        return pltpu.VMEM(shape, BF16)

    def dma(n):
        return pltpu.SemaphoreType.DMA((n,))

    return pl.pallas_call(
        layer_kernel,
        out_shape=(
            jax.ShapeDtypeStruct((rows, width), BF16),
            jax.ShapeDtypeStruct((rows, width), BF16),
        ),
        in_specs=[smem] * 2 + [vmem] * 7 + [hbm] * 4,
        out_specs=(vmem, vmem),
        scratch_shapes=[
            buf(pool, 2, page, head_width),
            buf(experts, head_width, width),
            pltpu.VMEM((TOPA, tokens, head_width), F32),
            buf(tokens, experts * head_width),
            buf(nz, rows, width),
            buf(nz - 1, rows, width),
            buf(nz, cap, width),
            buf(nz - 1, cap, width),
            buf(2, 4, block, half_cols),
            buf(2, 4, block, half_cols),
            buf(units, width),
            buf(units, width),
            buf(units, width),
            buf(4, 2 * block, units),
            buf(2, 4, block, half_cols),
            buf(2, 4, block, half_cols),
            buf(2, 2, block // 2, half_cols),
            buf(2, 2, block, half_cols),
            buf(block, half_cols),
            buf(block, half_cols),
            buf(4, block, half_cols),
            buf(2, block // 2, half_cols),
            buf(2, block, half_cols),
            buf(nz, cap, width),
            buf(nz - 1, cap, width),
            dma(1), dma(experts),
            dma(4 * (nz - 1)), dma(4 * (nz - 1)), dma(2 * (nz - 1)), dma(2 * (nz - 1)),
            dma(17), dma(17), dma(17), dma(17), dma(9), dma(9), dma(3),
        ],
        compiler_params=pltpu.CompilerParams(
            collective_id=0, has_side_effects=True, vmem_limit_bytes=VMEM_LIMIT
        ),
        name="layer",
    )(
        table, lengths, q, head_route, head_gate, residual, gain, route, egate,
        kv_cache, out_weight, gate_up, down,
    )


def local(
    residual, queries, kv_cache, page_table, seq_lengths, head_route, head_gate, out_weight,
    norm_gain, expert_route, expert_gate, gate_up, down_weight,
):
    return layer(
        page_table, seq_lengths, jnp.transpose(queries, (1, 0, 2)), head_route.T, head_gate.T,
        residual, norm_gain.reshape(1, -1), expert_route.T, expert_gate.T,
        kv_cache, out_weight, jnp.transpose(gate_up[0], (0, 2, 1)), down_weight[0],
    )


def solution(mesh):
    return jax.shard_map(
        local,
        mesh=mesh,
        in_specs=(
            P(("req", "exp"), None),
            P("req", None, "exp"),
            P("req", None, None, "exp"),
            P("req", None),
            P("req"),
            P("req", None),
            P("req", None),
            P(None, "exp", None),
            P(),
            P(("req", "exp"), None),
            P(("req", "exp"), None),
            P("exp", None, None, "req"),
            P("exp", "req", None),
        ),
        out_specs=(P(("req", "exp"), None), P(("req", "exp"), None)),
        check_vma=False,
    )
```

```python
import jax
import jax.numpy as jnp
from jax import lax
from jax.experimental import pallas as pl
from jax.experimental.pallas import tpu as pltpu
from jax.sharding import PartitionSpec as P

HD = 128
TOPA = 2
SPAN = 120
F32 = jnp.float32
BF16 = jnp.bfloat16
MESH = pl.DeviceIdType.MESH
VMEM_LIMIT = 60 * 1024 * 1024


def column(row):
    n = row.shape[1]
    same = lax.broadcasted_iota(jnp.int32, (n, n), 0) == lax.broadcasted_iota(jnp.int32, (n, n), 1)
    return jnp.sum(jnp.where(same, jnp.broadcast_to(row, (n, n)), 0.0), axis=1, keepdims=True)


def attend(q, k, v, allowed):
    scores = lax.dot_general(
        q, k, (((1,), (1,)), ((), ())), preferred_element_type=F32
    ) * HD ** (-0.5)
    scores = jnp.where(allowed, scores, -1e30)
    raised = jnp.exp(scores - jnp.max(scores, axis=1, keepdims=True))
    total = jnp.sum(raised, axis=1, keepdims=True)
    return jnp.dot(raised.astype(BF16), v, preferred_element_type=F32) / total


def layer_kernel(
    table, lengths, q_ref, head_route, head_gate, residual, gain, route, egate,
    kv_hbm, w_hbm, gu_hbm, d_hbm, attended_ref, mix_ref,
    qs, kv, w, mix, x_rows, partial, half_buf, rs_buf, out_buf, in_buf, ra, rb, wg, wu, wd, act, pa, pb,
    ta1, ta2, sa, ta3, tb1, tb2, tb3, ret_out, ret_in,
    kv_sem, o_sem, s_send, s_recv, z_send, z_recv, ag_send, ag_recv, rs_send, rs_recv,
    w_send, w_recv, l_sem,
):
    nz = partial.shape[0]
    rows = residual.shape[0]
    cap = out_buf.shape[1]
    block = nz * cap
    half_cols = ra.shape[3]
    hidden = d_hbm.shape[0]
    me = lax.axis_index("req")
    z = lax.axis_index("exp")
    c = lax.rem(me, 2)
    y = lax.rem(lax.div(me, 2), 4)
    x = lax.div(me, 8)
    xp, xm, x2 = lax.rem(x + 1, 4), lax.rem(x + 3, 4), lax.rem(x + 2, 4)
    yw = y + 1 - 2 * lax.rem(y, 2)
    turned = lax.rem(y + 3, 4)
    ys = lax.rem(turned, 2)
    yo = 1 - ys
    yr = lax.rem(turned + 1 - 2 * ys + 1, 4)

    def dev(x_, y_, c_):
        return ((x_ * 4 + y_) * 2 + c_, z)

    right, left = dev(xp, y, c), dev(xm, y, c)
    pair = dev(x, yr, c)
    w_pair = dev(x, yw, c)
    core = dev(x, y, 1 - c)

    def ahead(d):
        return (me, lax.rem(z + d, nz))

    def behind(d):
        return (me, lax.rem(z + nz - d, nz))

    barrier = pltpu.get_barrier_semaphore()
    others = [ahead(d) for d in range(1, nz)] + [right, left, pair, w_pair, core]
    for other in others:
        pl.semaphore_signal(barrier, inc=1, device_id=other, device_id_type=MESH)
    kv_copy = pltpu.make_async_copy(kv_hbm, kv, kv_sem.at[0])
    kv_copy.start()
    experts = w.shape[0]
    o_copies = [pltpu.make_async_copy(w_hbm.at[e], w.at[e], o_sem.at[e]) for e in range(experts)]
    for copy in o_copies:
        copy.start()
    pages = table.shape[1]
    decodes = table.shape[0] - 1
    page = kv.shape[2]
    width = q_ref.shape[2]
    tokens = q_ref.shape[0]
    keys = pages * page
    row_pos = lengths[0] - SPAN + lax.broadcasted_iota(jnp.int32, (tokens, keys), 0)
    causal = lax.broadcasted_iota(jnp.int32, (tokens, keys), 1) <= row_pos
    tail = 2 * decodes
    d_keys = decodes * page
    d_row = lax.broadcasted_iota(jnp.int32, (TOPA * tail, d_keys), 0) % tail - decodes
    d_col = lax.broadcasted_iota(jnp.int32, (TOPA * tail, d_keys), 1)
    d_slot = d_col // page
    length_of = jnp.zeros((TOPA * tail, d_keys), jnp.int32)
    for s in range(decodes):
        length_of = jnp.where(d_slot == s, lengths[s + 1], length_of)
    d_allowed = (d_slot == d_row) & (d_col % page < length_of)
    pl.semaphore_wait(barrier, len(others))

    started = []

    def send(src, dst, sems, i, device):
        copy = pltpu.make_async_remote_copy(
            src_ref=src, dst_ref=dst, send_sem=sems[0].at[i], recv_sem=sems[1].at[i],
            device_id=device, device_id_type=MESH,
        )
        copy.start()
        started.append(copy)
        return copy

    zs, ags, rss, ws = (z_send, z_recv), (ag_send, ag_recv), (rs_send, rs_recv), (w_send, w_recv)
    ss = (s_send, s_recv)
    far_first = (4, 3, 5, 2, 6, 1, 7)

    a_cols, b_cols, all_cols = pl.ds(0, half_cols), pl.ds(half_cols, half_cols), slice(None)
    parts = (
        (gu_hbm.at[0], wg, all_cols), (gu_hbm.at[1], wu, all_cols),
        (d_hbm, wd, b_cols), (d_hbm, wd, a_cols),
    )

    def source(i):
        return parts[i][0].at[:, parts[i][2]]

    def part(i, b):
        return parts[i][1].at[pl.ds(b * hidden, hidden), parts[i][2]]

    w_y = [send(source(i), part(i, 1), ws, i, w_pair) for i in range(4)]
    w_c = [send(source(i), part(i, 2), ws, 4 + i, core) for i in range(4)]
    w_l = [pltpu.make_async_copy(source(i), part(i, 0), l_sem.at[i]) for i in range(4)]
    for copy in w_l:
        copy.start()

    for t in range(TOPA):
        qs[t] = q_ref[:, t, :]
    kv_copy.wait()
    for h in range(width // HD):
        cols = slice(h * HD, (h + 1) * HD)

        def paged(kind, spots):
            return jnp.concatenate([kv[table[s, p], kind, :, cols] for s, p in spots], axis=0)

        pre = [(0, p) for p in range(pages)]
        k_pre, v_pre = paged(0, pre), paged(1, pre)
        for t in range(TOPA):
            mix[t, :, cols] = attend(qs[t, :, cols], k_pre, v_pre, causal)
        dec = [(s + 1, 0) for s in range(decodes)]
        k_dec, v_dec = paged(0, dec), paged(1, dec)
        q_dec = jnp.concatenate(
            [qs[t, tokens - tail : tokens, cols] for t in range(TOPA)], axis=0
        )
        o_dec = attend(q_dec, k_dec, v_dec, d_allowed)
        for t in range(TOPA):
            mix[t, SPAN:tokens, cols] = o_dec[t * tail + decodes : (t + 1) * tail]
    mixes = [mix[t].astype(BF16).astype(F32) for t in range(TOPA)]
    routes = [column(head_route[t : t + 1].astype(F32)) for t in range(TOPA)]
    gates = [column(head_gate[t : t + 1]) for t in range(TOPA)]
    for e in range(experts):
        gated = jnp.zeros((tokens, width), F32)
        for t in range(TOPA):
            gated = gated + jnp.where(routes[t] == e, gates[t], 0.0) * mixes[t]
        x_rows[:, e * width : (e + 1) * width] = gated.astype(BF16)
    for copy in o_copies:
        copy.wait()

    outs = w.shape[2]
    chunk = outs // 4
    scatter, halves = [], []

    def block_cols(k, part_of):
        return pl.ds(k * chunk + part_of * (chunk // 2), chunk // 2)

    def scatter_send(k, d):
        cols = pl.ds(k * chunk, chunk)
        scatter.append(
            send(
                partial.at[lax.rem(z + d, nz), :, cols], rs_buf.at[d - 1, :, cols],
                ss, k * nz + d - 1, ahead(d),
            )
        )

    def pass_on(k):
        for side, d in ((0, nz // 2 - 1), (1, nz // 2 + 1)):
            halves[2 * k + side].wait_recv()
            spot, cols = lax.rem(z + d, nz), block_cols(k, side)
            partial[spot, :, cols] = (
                partial[spot, :, cols].astype(F32) + half_buf[side, :, cols].astype(F32)
            ).astype(BF16)
            scatter_send(k, d)

    for k in range(outs // chunk):
        partial[:, :, k * chunk : (k + 1) * chunk] = jnp.dot(
            x_rows[...],
            w[:, :, k * chunk : (k + 1) * chunk].reshape(experts * width, chunk),
            preferred_element_type=F32,
        ).astype(BF16).reshape(nz, rows, chunk)
        far = lax.rem(z + nz // 2, nz)
        for side, device in ((0, ahead(1)), (1, behind(1))):
            cols = block_cols(k, side)
            halves.append(
                send(
                    partial.at[far, :, cols], half_buf.at[side, :, cols],
                    ss, k * nz + (nz // 2 - 1 if side == 0 else nz - 1), device,
                )
            )
        for d in (2, 6, 1, 7):
            scatter_send(k, d)
        if k > 0:
            pass_on(k - 1)
    pass_on(outs // chunk - 1)

    def routed(t):
        rel = column(route[t : t + 1].astype(F32)) - z.astype(F32)
        rel = jnp.where(rel < 0, rel + nz, rel)
        spot = lax.broadcasted_iota(jnp.int32, (rows, block), 1) // cap
        return rel == spot.astype(F32)

    named = [routed(t) for t in range(TOPA)]
    member = jnp.where(named[0] | named[1], 1.0, 0.0).astype(F32)
    lower = jnp.where(
        lax.broadcasted_iota(jnp.int32, (rows, rows), 1)
        < lax.broadcasted_iota(jnp.int32, (rows, rows), 0),
        1.0, 0.0,
    ).astype(BF16)
    rank = jnp.dot(lower, member.astype(BF16), preferred_element_type=F32)
    place = (lax.broadcasted_iota(jnp.int32, (rows, block), 1) % cap).astype(F32)
    placing = jnp.where(rank == place, member, 0.0)
    egates = [column(egate[t : t + 1]) for t in range(TOPA)]

    for copy in scatter:
        copy.wait_recv()
    summed = residual[...].astype(F32) + partial[z].astype(F32)
    for d in range(1, nz):
        if d != nz // 2:
            summed = summed + rs_buf[d - 1].astype(F32)
    attended = summed.astype(BF16)
    attended_ref[...] = attended
    values = attended.astype(F32)
    normed = (
        values
        * lax.rsqrt(jnp.mean(values * values, axis=1, keepdims=True) + 1e-06)
        * gain[...]
    ).astype(BF16)
    outgoing = lax.dot_general(
        placing.astype(BF16), normed, (((0,), (0,)), ((), ())), preferred_element_type=F32
    )
    for d in range(nz):
        out_buf[d] = outgoing[d * cap : (d + 1) * cap].astype(BF16)
    dispatch = [
        send(out_buf.at[d], in_buf.at[d - 1], zs, d - 1, ahead(d)) for d in far_first
    ]
    for copy in dispatch:
        copy.wait_recv()
    arrived = jnp.concatenate(
        [out_buf[0].astype(F32)] + [in_buf[d].astype(F32) for d in range(nz - 1)], axis=0
    ).astype(BF16)

    ra[ys, x] = arrived[:, :half_cols]
    rb[ys, x] = arrived[:, half_cols:]
    mid = block // 2
    low_rows, high_rows = pl.ds(0, mid), pl.ds(mid, mid)

    def forward(buffer, i, device, *spot):
        return send(buffer.at[spot], buffer.at[spot], ags, i, device)

    a_y = forward(ra, 0, pair, ys, x)
    b_r = forward(rb, 1, right, ys, x)
    b_l = forward(rb, 2, left, ys, x)
    a_r = forward(ra, 3, right, ys, x)
    a_l = forward(ra, 4, left, ys, x)
    b_y = forward(rb, 5, pair, ys, x)
    w_d = []

    def relay_weights(i):
        w_y[i].wait_recv()
        w_d.append(send(part(i, 1), part(i, 3), ws, 8 + i, core))

    def have_weights(i):
        w_c[i].wait_recv()
        w_d[i].wait_recv()
        w_l[i].wait()

    relay_weights(0)
    b_r.wait_recv()
    b_r2 = forward(rb, 6, right, ys, xm, low_rows)
    b_ym = forward(rb, 7, pair, ys, xm)
    b_l.wait_recv()
    b_l2 = forward(rb, 8, left, ys, xp, high_rows)
    b_yp = forward(rb, 9, pair, ys, xp)
    a_y.wait_recv()
    a_or = forward(ra, 10, right, yo, x)
    a_ol = forward(ra, 11, left, yo, x)
    relay_weights(1)
    a_r.wait_recv()
    a_r2 = forward(ra, 12, right, ys, xm, low_rows)
    a_l.wait_recv()
    a_l2 = forward(ra, 13, left, ys, xp, high_rows)
    b_r2.wait_recv()
    b_l2.wait_recv()
    b_y2 = forward(rb, 14, pair, ys, x2)

    units = act.shape[2]
    step = 256

    def wide(x_half, w_half):
        return lax.dot_general(
            x_half, w_half, (((1,), (1,)), ((), ())), preferred_element_type=F32
        )

    def up_project(spot):
        xa = ra[:, spot].reshape(2 * block, half_cols)
        xb = rb[:, spot].reshape(2 * block, half_cols)
        for n in range(0, units, step):
            size = min(step, units - n)
            here = slice(n, n + size)
            gate_part = wide(xa, wg[here, :half_cols]) + wide(xb, wg[here, half_cols:])
            up_part = wide(xa, wu[here, :half_cols]) + wide(xb, wu[here, half_cols:])
            act[spot, :, here] = (
                gate_part / (1.0 + jnp.exp(-gate_part)) * up_part
            ).astype(BF16)

    def down_project(store, base, spot):
        for n in range(0, half_cols, 2 * step):
            store[:, spot, :, n : n + 2 * step] = jnp.dot(
                act[spot], wd[:, base + n : base + n + 2 * step], preferred_element_type=F32
            ).astype(BF16).reshape(2, block, 2 * step)

    have_weights(0)
    have_weights(1)
    b_y.wait_recv()
    up_project(x)
    a_or.wait_recv()
    a_or2 = forward(ra, 15, right, yo, xm, low_rows)
    a_ol.wait_recv()
    a_ol2 = forward(ra, 16, left, yo, xp, high_rows)
    b_ym.wait_recv()
    up_project(xm)
    relay_weights(2)
    b_yp.wait_recv()
    up_project(xp)
    for copy in (a_r2, a_l2, a_or2, a_ol2, b_y2):
        copy.wait_recv()
    up_project(x2)

    have_weights(2)
    b1 = []
    for n, spot in enumerate((x2, xp, xm, x)):
        down_project(pb, half_cols, spot)
        b1.append(send(pb.at[yo, spot], tb1.at[n], rss, n, pair))

    def add(store, term, *spot):
        store[spot] = (store[spot].astype(F32) + term.astype(F32)).astype(BF16)

    low, high = slice(0, mid), slice(mid, block)
    relay_weights(3)
    b1[0].wait_recv()
    add(pb, tb1[0], ys, x2)
    b2r = send(pb.at[ys, x2, low_rows], tb2.at[0], rss, 4, right)
    b2l = send(pb.at[ys, x2, high_rows], tb2.at[1], rss, 5, left)
    have_weights(3)
    down_project(pa, 0, x2)
    a1r = send(pa.at[yo, x2, low_rows], ta1.at[0, 0], rss, 6, right)
    a1l = send(pa.at[yo, x2, high_rows], ta1.at[0, 1], rss, 7, left)
    a1rs = send(pa.at[ys, x2, low_rows], ta1.at[1, 0], rss, 8, right)
    a1ls = send(pa.at[ys, x2, high_rows], ta1.at[1, 1], rss, 9, left)
    down_project(pa, 0, xp)
    down_project(pa, 0, xm)
    a1r.wait_recv()
    add(pa, ta1[0, 0], yo, xp, low)
    a2r = send(pa.at[yo, xp], ta2.at[0, 0], rss, 10, right)
    a1l.wait_recv()
    add(pa, ta1[0, 1], yo, xm, high)
    a2l = send(pa.at[yo, xm], ta2.at[0, 1], rss, 11, left)
    a1rs.wait_recv()
    add(pa, ta1[1, 0], ys, xp, low)
    a2rs = send(pa.at[ys, xp], ta2.at[1, 0], rss, 12, right)
    a1ls.wait_recv()
    add(pa, ta1[1, 1], ys, xm, high)
    a2ls = send(pa.at[ys, xm], ta2.at[1, 1], rss, 13, left)
    b1[1].wait_recv()
    add(pb, tb1[1], ys, xp)
    b1[2].wait_recv()
    add(pb, tb1[2], ys, xm)
    b2r.wait_recv()
    add(pb, tb2[0], ys, xp, low)
    b3r = send(pb.at[ys, xp], tb3.at[0], rss, 14, right)
    b2l.wait_recv()
    add(pb, tb2[1], ys, xm, high)
    b3l = send(pb.at[ys, xm], tb3.at[1], rss, 15, left)
    down_project(pa, 0, x)
    a2r.wait_recv()
    a2l.wait_recv()
    sa[...] = (
        pa[yo, x].astype(F32) + ta2[0, 0].astype(F32) + ta2[0, 1].astype(F32)
    ).astype(BF16)
    a3 = send(sa, ta3, rss, 16, pair)
    a2rs.wait_recv()
    a2ls.wait_recv()
    final_a = pa[ys, x].astype(F32) + ta2[1, 0].astype(F32) + ta2[1, 1].astype(F32)
    a3.wait_recv()
    final_a = final_a + ta3[...].astype(F32)
    b1[3].wait_recv()
    final_b = pb[ys, x].astype(F32) + tb1[3].astype(F32)
    b3r.wait_recv()
    b3l.wait_recv()
    final_b = final_b + tb3[0].astype(F32) + tb3[1].astype(F32)

    for d in range(nz):
        ret_out[d, :, :half_cols] = final_a[d * cap : (d + 1) * cap].astype(BF16)
        ret_out[d, :, half_cols:] = final_b[d * cap : (d + 1) * cap].astype(BF16)
    home = [
        send(ret_out.at[d], ret_in.at[d - 1], zs, nz - 2 + d, behind(d)) for d in far_first
    ]
    weights = jnp.where(named[0], egates[0], 0.0) + jnp.where(named[1], egates[1], 0.0)
    weights = placing * weights
    coarse = weights.astype(BF16)
    fine = (weights - coarse.astype(F32)).astype(BF16)
    both = jnp.concatenate([coarse, fine], axis=0)
    for copy in home:
        copy.wait_recv()
    back = jnp.concatenate(
        [ret_out[0].astype(F32)] + [ret_in[d].astype(F32) for d in range(nz - 1)], axis=0
    ).astype(BF16)
    mixed = jnp.dot(both, back, preferred_element_type=F32)
    mix_ref[...] = (mixed[:rows] + mixed[rows:]).astype(BF16)
    for copy in started:
        copy.wait_send()


def layer(
    table, lengths, q, head_route, head_gate, residual, gain, route, egate,
    kv_cache, out_weight, gate_up, down,
):
    pool, _, page, head_width = kv_cache.shape
    experts = out_weight.shape[0]
    tokens = q.shape[0]
    rows, width = residual.shape
    nz = tokens // rows
    half_cols = width // 2
    hidden = down.shape[0]
    cap = max(2, 2 * TOPA * rows // nz)
    block = nz * cap
    units = 4 * hidden
    vmem = pl.BlockSpec(memory_space=pltpu.VMEM)
    smem = pl.BlockSpec(memory_space=pltpu.SMEM)
    hbm = pl.BlockSpec(memory_space=pl.ANY)

    def buf(*shape):
        return pltpu.VMEM(shape, BF16)

    def dma(n):
        return pltpu.SemaphoreType.DMA((n,))

    return pl.pallas_call(
        layer_kernel,
        out_shape=(
            jax.ShapeDtypeStruct((rows, width), BF16),
            jax.ShapeDtypeStruct((rows, width), BF16),
        ),
        in_specs=[smem] * 2 + [vmem] * 7 + [hbm] * 4,
        out_specs=(vmem, vmem),
        scratch_shapes=[
            buf(TOPA, tokens, head_width),
            buf(pool, 2, page, head_width),
            buf(experts, head_width, width),
            pltpu.VMEM((TOPA, tokens, head_width), F32),
            buf(tokens, experts * head_width),
            buf(nz, rows, width),
            buf(2, rows, width),
            buf(nz - 1, rows, width),
            buf(nz, cap, width),
            buf(nz - 1, cap, width),
            buf(2, 4, block, half_cols),
            buf(2, 4, block, half_cols),
            buf(units, width),
            buf(units, width),
            buf(units, width),
            buf(4, 2 * block, units),
            buf(2, 4, block, half_cols),
            buf(2, 4, block, half_cols),
            buf(2, 2, block // 2, half_cols),
            buf(2, 2, block, half_cols),
            buf(block, half_cols),
            buf(block, half_cols),
            buf(4, block, half_cols),
            buf(2, block // 2, half_cols),
            buf(2, block, half_cols),
            buf(nz, cap, width),
            buf(nz - 1, cap, width),
            dma(1), dma(experts),
            dma(4 * nz), dma(4 * nz), dma(2 * (nz - 1)), dma(2 * (nz - 1)),
            dma(17), dma(17), dma(17), dma(17), dma(12), dma(12), dma(4),
        ],
        compiler_params=pltpu.CompilerParams(
            collective_id=0, has_side_effects=True, vmem_limit_bytes=VMEM_LIMIT
        ),
        name="layer",
    )(
        table, lengths, q, head_route, head_gate, residual, gain, route, egate,
        kv_cache, out_weight, gate_up, down,
    )


def local(
    residual, queries, kv_cache, page_table, seq_lengths, head_route, head_gate, out_weight,
    norm_gain, expert_route, expert_gate, gate_up, down_weight,
):
    return layer(
        page_table, seq_lengths, queries, head_route.T, head_gate.T,
        residual, norm_gain.reshape(1, -1), expert_route.T, expert_gate.T,
        kv_cache, out_weight, jnp.transpose(gate_up[0], (0, 2, 1)), down_weight[0],
    )


def solution(mesh):
    return jax.shard_map(
        local,
        mesh=mesh,
        in_specs=(
            P(("req", "exp"), None),
            P("req", None, "exp"),
            P("req", None, None, "exp"),
            P("req", None),
            P("req"),
            P("req", None),
            P("req", None),
            P(None, "exp", None),
            P(),
            P(("req", "exp"), None),
            P(("req", "exp"), None),
            P("exp", None, None, "req"),
            P("exp", "req", None),
        ),
        out_specs=(P(("req", "exp"), None), P(("req", "exp"), None)),
        check_vma=False,
    )
```
